128 devices in a mesh: grp: 2 (over core), dev: 64 (over x, y, z).
Axes of the slice: x: 4, y: 4, z: 4, core: 2. Of those that a mesh axis runs over, the one named last changes fastest.
Arguments:
- residual_in: bfloat16 [2048, 2048], P(('grp', 'dev')), may hold values from -1.5 to 1.5
- queries: bfloat16 [2, 1024, 4096], P(None, 'dev', 'grp'), may hold values from -2.5 to 2.5
- latest_key_value: bfloat16 [2, 1024, 4, 256], P(None, 'dev', 'grp'), may hold values from -2.5 to 2.5
- key_value_cache: bfloat16 [2, 1024, 4, 256, 256], P(None, 'dev', 'grp'), may hold values from -2.5 to 2.5
- cache_len: int32 [2, 1024], P(None, 'dev'), may hold values from 1 to 256, 131072 in all within a row
- out_weight: bfloat16 [4096, 2048], P('grp'), may hold values from -0.09375 to 0.09375
- norm_gain: bfloat16 [2048], replicated, may hold values from 0.099609375 to 1.8984375
- router_weight: bfloat16 [2048, 128], replicated, may hold values from -0.125 to 0.125
- routes: int32 [2048, 8], P(('grp', 'dev')), may hold values from 0 to 127, all different within a row; in each aligned block of 16 rows (0 to 15, 16 to 31, ...) at most 2 rows name the same one
- expert_gate_up: bfloat16 [128, 2048, 1536], P(('grp', 'dev')), may hold values from -0.125 to 0.125
- expert_down: bfloat16 [128, 768, 2048], P(('grp', 'dev')), may hold values from -0.21875 to 0.21875
Outputs:
- layer_out: bfloat16 [2048, 2048], P(('grp', 'dev'))
The draws below stay inside these ranges and needn't reach their ends.
Inputs may be any that keep to these rules, and one draw needn't show every extreme that they name: Each row of cache_len of 1024 entries sums to 131072, and its largest entry is exactly 256. `routes`: the 8 experts of a row are distinct; in each aligned block of 16 rows (the rows of one device) no expert is named by more than 2 rows, a bound that some block reaches.
All inputs are finite; a program needn't handle non-finite values. No bound on the sum of `cache_len` on one device may be relied on, other than what follows from the above.
Results may differ from the reference program's by a relative error of at most 0.017.
Values may be sent and summed in bfloat16 or wider, within the bound.
No kernel may reach another device: no remote copies, remote signals or barrier semaphores. Data moves between devices by JAX's collectives and lax.ppermute only.
A program may use at most 128 MiB of HBM per device.

```python
import math
import jax
import jax.numpy as jnp
import numpy as np
from jax import lax

D = 2048
QUERY_HEADS = 32
KEY_VALUE_HEADS = 4
HEAD_SIZE = 128
FF = 768
TOPK = 8
CACHE_SLOTS_MAX = 256
TOK = 16
EXPERTS = 128
HALF_BATCH_ROWS = 1024
ROWS = 2048
CAP = 2


def block_levels(rng, dims, split, smallest, top_value):
    def one(dim, shards_of):
        heights = jax.random.uniform(jax.random.fold_in(jax.random.fold_in(rng, 6), dim), (shards_of,), jnp.float32, smallest / len(split), top_value / len(split))
        return jnp.repeat(jnp.exp(heights), dims[dim] // shards_of).reshape((-1,) + (1,) * (len(dims) - dim - 1))

    factor_of = one(*split[0])
    for cut in split[1:]:
        factor_of = factor_of * one(*cut)
    return factor_of


def profile(count, total, most, lean):
    portions = [(1 << 20) // math.isqrt(standing ** lean) + 1 for standing in range(2, count + 1)]
    spare, holding = total - most - (count - 1), [1] * (count - 1)
    while spare > 0:
        movable = [i for i in range(count - 1) if holding[i] < most]
        whole, budget = sum([portions[i] for i in movable]), spare
        for i in movable:
            more = min(most - holding[i], max(1, budget * portions[i] // whole), spare)
            holding[i] = holding[i] + more
            spare = spare - more
    return np.array([most] + holding)


def uneven_parts(key, amount, total, bound, lean):
    if amount == 2:
        one = jax.random.randint(key, (), max(1, total - bound), min(bound, total - 1) + 1)
        return jnp.stack([one, total - one])
    sizes = jnp.asarray(profile(amount, total, bound, lean), jnp.int32)
    pairs = (amount - 1) // 2
    giver, taker = sizes[1:1 + 2 * pairs:2], sizes[2:2 + 2 * pairs:2]
    margin = jnp.minimum(giver - 1, bound - taker)
    passed = jax.random.randint(jax.random.fold_in(key, 1), (pairs,), 0, 1 << 20) % (margin + 1)
    sizes = sizes.at[1:1 + 2 * pairs:2].set(giver - passed).at[2:2 + 2 * pairs:2].set(taker + passed)
    return sizes[jax.random.permutation(jax.random.fold_in(key, 2), amount)]


def assign_block(key, own, number, rows, amount, top, reach, skew):
    sequence = jax.random.permutation(key, amount)
    heavy_load, common = load_shares(amount, rows * top, reach, skew, True), load_shares(amount, rows * top, reach, skew, False)
    places = jnp.arange(amount)

    def named(sizes, offset_by):
        used = int((sizes > 0).sum())
        fixed = max(1, used // 4)
        moved = fixed + (places - fixed + offset_by * (used - fixed)) % max(1, amount - fixed)
        return jnp.zeros((amount,), jnp.int32).at[sequence[jnp.where(places < fixed, places, moved)]].set(jnp.asarray(sizes, jnp.int32))

    sizes = jnp.where(number % 4 == 0, named(heavy_load, number // 4), named(common, number - number // 4 - 1))
    mixed = jax.random.permutation(jax.random.fold_in(own, 3), amount)
    donor, receiver = mixed[0:amount // 2 * 2:2], mixed[1:amount // 2 * 2:2]
    room = jnp.minimum(sizes[donor] - 1, reach - sizes[receiver]) // 2
    room = jnp.where((donor == sequence[0]) | (receiver == sequence[0]) | (sizes[receiver] == 0), 0, jnp.maximum(room, 0))
    moved = jax.random.randint(jax.random.fold_in(own, 4), (amount // 2,), 0, 1 << 20) % (room + 1)
    sizes = sizes.at[donor].add(-moved).at[receiver].add(moved)
    items = jnp.searchsorted(jnp.cumsum(sizes), jnp.arange(rows * top), side="right").astype(jnp.int32)
    table = items.reshape(top, rows).T
    table = table[jax.random.permutation(jax.random.fold_in(own, 1), rows)]
    offset_by = jax.random.randint(jax.random.fold_in(own, 2), (rows, 1), 0, top)
    return jnp.take_along_axis(table, (jnp.arange(top)[None, :] + offset_by) % top, axis=1)


def load_shares(count, total, limit, skew, full):
    loads = [(1 << 20) // math.isqrt(standing ** skew) + 1 for standing in range(1, count + 1)]
    largest = limit if full else min(limit, max(-(-total // count), total * loads[0] // sum(loads)))
    least = 1 if total - largest >= count - 1 else 0
    holding, spare = [largest] + [least] * (count - 1), total - largest - least * (count - 1)
    while spare > 0:
        movable = [i for i in range(1, count) if holding[i] < largest] or [i for i in range(1, count) if holding[i] < limit]
        pool, remaining = sum([loads[i] for i in movable]), spare
        for i in movable:
            more = min(limit - holding[i], max(1, remaining * loads[i] // pool), spare)
            holding[i] = holding[i] + more
            spare = spare - more
    return np.array(holding)


def gaussian(stream_key, extent, spread, bound, shards=(), kind=jnp.bfloat16):
    array = jax.random.normal(stream_key, extent, jnp.float32) * spread
    if len(shards) > 0:
        array = block_levels(stream_key, extent, shards, -0.22, 0.18) * array
    return jnp.clip(array, min=-bound, max=bound).astype(kind)


def setup_inputs(seed: int = 0) -> dict:
    streams_of = jax.random.split(jax.random.key(seed), 12)
    residual_in = gaussian(streams_of[0], (ROWS, D), 0.1, 1.5, ((0, 128),))
    queries = gaussian(streams_of[1], (2, HALF_BATCH_ROWS, QUERY_HEADS * HEAD_SIZE), 1.0, 2.5, ((1, 64), (2, 2)))
    latest_key_value = gaussian(streams_of[2], (2, HALF_BATCH_ROWS, KEY_VALUE_HEADS, 2 * HEAD_SIZE), 1.0, 2.5, ((1, 64), (2, 2)))
    key_value_cache = gaussian(streams_of[3], (2, HALF_BATCH_ROWS, KEY_VALUE_HEADS, CACHE_SLOTS_MAX, 2 * HEAD_SIZE), 1.0, 2.5, ((1, 64), (2, 2)))
    cache_len = jax.vmap(lambda own: uneven_parts(own, HALF_BATCH_ROWS, HALF_BATCH_ROWS * CACHE_SLOTS_MAX // 2, CACHE_SLOTS_MAX, 2))(jax.random.split(streams_of[4], 2)).reshape((2, HALF_BATCH_ROWS)).astype(jnp.int32)
    out_weight = gaussian(streams_of[5], (QUERY_HEADS * HEAD_SIZE, D), (QUERY_HEADS * HEAD_SIZE) ** -0.5, 0.09375, ((0, 2),))
    norm_gain = jnp.clip(1.0 + 0.18 * jax.random.normal(streams_of[6], (D,), jnp.float32), 0.099609375, 1.8984375).astype(jnp.bfloat16)
    router_weight = gaussian(streams_of[7], (D, EXPERTS), D ** -0.5, 0.125)
    routes_keys = jax.random.split(jax.random.fold_in(streams_of[8], 1), ROWS // TOK)
    routes_turns = jax.random.permutation(jax.random.fold_in(streams_of[8], 3), ROWS // TOK)
    routes = jax.vmap(lambda own, number: assign_block(jax.random.fold_in(streams_of[8], 2), own, number, TOK, EXPERTS, TOPK, CAP, 2))(routes_keys, routes_turns).reshape((ROWS, TOPK))
    expert_gate_up = gaussian(streams_of[9], (EXPERTS, D, 2 * FF), D ** -0.5, 0.125, ((0, 128),))
    expert_down = gaussian(streams_of[10], (EXPERTS, FF, D), FF ** -0.5, 0.21875, ((0, 128),))
    return dict(residual_in=residual_in, queries=queries, latest_key_value=latest_key_value, key_value_cache=key_value_cache, cache_len=cache_len, out_weight=out_weight, norm_gain=norm_gain, router_weight=router_weight, routes=routes, expert_gate_up=expert_gate_up, expert_down=expert_down)


def attend_half(query_vector, fresh, cache, lengths):
    batch_rows = query_vector.shape[0]
    query_group = QUERY_HEADS // KEY_VALUE_HEADS
    query_stack = query_vector.astype(jnp.float32).reshape(batch_rows, KEY_VALUE_HEADS, query_group, HEAD_SIZE)
    scale = 1.0 / math.sqrt(HEAD_SIZE)
    visible = jnp.arange(CACHE_SLOTS_MAX, dtype=jnp.int32)[None, None, :] < lengths[:, None, None]

    def single_head(head):
        cache_head = lax.dynamic_index_in_dim(cache, head, 1, keepdims=False).astype(jnp.float32)
        fresh_head = lax.dynamic_index_in_dim(fresh, head, 1, keepdims=False).astype(jnp.float32)
        query_head = lax.dynamic_index_in_dim(query_stack, head, 1, keepdims=False)
        scores = jnp.einsum('rgd,rsd->rgs', query_head, cache_head[:, :, :HEAD_SIZE]) * scale
        own_score = jnp.einsum('rgd,rd->rg', query_head, fresh_head[:, :HEAD_SIZE]) * scale
        raised = jnp.where(visible, jnp.exp(scores), 0.0)
        own_raised = jnp.exp(own_score)
        totals = lax.optimization_barrier(jnp.sum(raised, axis=-1)) + own_raised
        weights = lax.optimization_barrier((raised / totals[:, :, None]).astype(jnp.bfloat16)).astype(jnp.float32)
        own_weight = lax.optimization_barrier((own_raised / totals).astype(jnp.bfloat16)).astype(jnp.float32)
        mixed = jnp.einsum('rgs,rsd->rgd', weights, cache_head[:, :, HEAD_SIZE:])
        return mixed + own_weight[:, :, None] * fresh_head[:, None, HEAD_SIZE:]
    head_list = lax.map(single_head, jnp.arange(KEY_VALUE_HEADS, dtype=jnp.int32))
    return jnp.transpose(head_list, (1, 0, 2, 3)).reshape(batch_rows, QUERY_HEADS * HEAD_SIZE).astype(jnp.bfloat16)

def reference(residual_in, queries, latest_key_value, key_value_cache, cache_len, out_weight, norm_gain, router_weight, routes, expert_gate_up, expert_down):
    attended = jnp.concatenate([attend_half(queries[index], latest_key_value[index], key_value_cache[index], cache_len[index]) for index in range(2)], axis=0)
    projected = jnp.dot(attended, out_weight, preferred_element_type=jnp.float32)
    hidden = residual_in.astype(jnp.float32) + projected
    meansq = lax.optimization_barrier(jnp.mean(hidden * hidden, axis=-1, keepdims=True))
    normed = (hidden * lax.rsqrt(meansq + 1e-06) * norm_gain.astype(jnp.float32)).astype(jnp.bfloat16)
    logits = jnp.dot(normed, router_weight, preferred_element_type=jnp.float32)
    picked = jnp.exp(jnp.take_along_axis(logits, routes, axis=1))
    gates = picked / lax.optimization_barrier(jnp.sum(picked, axis=1, keepdims=True))
    sources = ROWS // TOK
    assigned = TOK * TOPK
    flat_routes = routes.reshape(sources, assigned)
    onehot = (flat_routes[:, :, None] == jnp.arange(EXPERTS, dtype=jnp.int32)[None, None, :]).astype(jnp.int32)
    ranks = lax.optimization_barrier(jnp.sum(onehot * (jnp.cumsum(onehot, axis=1) - 1), axis=2)).astype(jnp.int32)
    target = (flat_routes * CAP + ranks).astype(jnp.int32)
    repeated = jnp.repeat(normed.reshape(sources, TOK, D), TOPK, axis=1)

    def place(targets, values):
        return jnp.zeros((EXPERTS * CAP, D), jnp.bfloat16).at[targets].set(values)
    slots = jax.vmap(place)(target, repeated).reshape(sources, EXPERTS, CAP, D)

    def one_expert(expert):
        inputs = lax.dynamic_index_in_dim(slots, expert, 1, keepdims=False).reshape(sources * CAP, D)
        weight_in = lax.dynamic_index_in_dim(expert_gate_up, expert, 0, keepdims=False)
        weight_out = lax.dynamic_index_in_dim(expert_down, expert, 0, keepdims=False)
        gate_up = jnp.dot(inputs, weight_in, preferred_element_type=jnp.float32)
        active = (jax.nn.silu(gate_up[:, :FF]) * gate_up[:, FF:]).astype(jnp.bfloat16)
        result = jnp.dot(active, weight_out, preferred_element_type=jnp.float32).astype(jnp.bfloat16)
        return result.reshape(sources, CAP, D)
    served = lax.map(one_expert, jnp.arange(EXPERTS, dtype=jnp.int32))
    returned = jnp.transpose(served, (1, 0, 2, 3)).reshape(sources, EXPERTS * CAP, D)
    picked_rows = jax.vmap(lambda table, position: table[position])(returned, target)
    picked_rows = picked_rows.reshape(ROWS, TOPK, D).astype(jnp.float32)
    combined = lax.optimization_barrier(jnp.sum(gates[:, :, None] * picked_rows, axis=1))
    return (hidden + combined).astype(jnp.bfloat16)
```

```python
import math

import jax
import jax.numpy as jnp
from jax import lax
from jax.sharding import PartitionSpec as P

HEAD_SIZE = 128
FF = 768


def per_device(
    residual_in,
    queries,
    latest_key_value,
    key_value_cache,
    cache_len,
    out_weight,
    norm_gain,
    router_weight,
    routes,
    expert_gate_up,
    expert_down,
):
    halves = queries.shape[0]
    tokens = queries.shape[1]
    kv_heads = key_value_cache.shape[2]
    positions = key_value_cache.shape[3]
    q_heads = queries.shape[2] // HEAD_SIZE
    query_group = q_heads // kv_heads
    width = residual_in.shape[1]
    scale = 1.0 / math.sqrt(HEAD_SIZE)
    query_vector = queries.reshape(halves, tokens, kv_heads, query_group, HEAD_SIZE)
    scores = (
        jnp.einsum(
            "hrkgd,hrksd->hrkgs",
            query_vector,
            key_value_cache[..., :HEAD_SIZE],
            preferred_element_type=jnp.float32,
        )
        * scale
    )
    own_score = (
        jnp.einsum(
            "hrkgd,hrkd->hrkg",
            query_vector,
            latest_key_value[..., :HEAD_SIZE],
            preferred_element_type=jnp.float32,
        )
        * scale
    )
    visible = (
        jnp.arange(positions, dtype=jnp.int32)[None, None, None, None, :]
        < cache_len[:, :, None, None, None]
    )
    raised = jnp.where(visible, jnp.exp(scores), 0.0)
    own_raised = jnp.exp(own_score)
    totals = jnp.sum(raised, axis=-1) + own_raised
    weights = (raised / totals[..., None]).astype(jnp.bfloat16)
    own_weight = (own_raised / totals).astype(jnp.bfloat16)
    mixed = jnp.einsum(
        "hrkgs,hrksd->hrkgd",
        weights,
        key_value_cache[..., HEAD_SIZE:],
        preferred_element_type=jnp.float32,
    )
    mixed = (
        mixed
        + own_weight.astype(jnp.float32)[..., None]
        * latest_key_value[..., HEAD_SIZE:].astype(jnp.float32)[:, :, :, None, :]
    )
    attended = mixed.astype(jnp.bfloat16).reshape(halves * tokens, q_heads * HEAD_SIZE)
    partial_value = jnp.dot(attended, out_weight, preferred_element_type=jnp.float32).reshape(
        halves, tokens, width
    )
    half = lax.axis_index("grp")
    kept = lax.dynamic_index_in_dim(partial_value, half, 0, keepdims=False)
    passed = lax.dynamic_index_in_dim(partial_value, 1 - half, 0, keepdims=False)
    projected = kept + lax.ppermute(passed, "grp", [(0, 1), (1, 0)])
    hidden = residual_in.astype(jnp.float32) + projected
    meansq = jnp.mean(hidden * hidden, axis=-1, keepdims=True)
    normed = (hidden * lax.rsqrt(meansq + 1e-06) * norm_gain.astype(jnp.float32)).astype(
        jnp.bfloat16
    )
    logits = jnp.dot(normed, router_weight, preferred_element_type=jnp.float32)
    picked = jnp.exp(jnp.take_along_axis(logits, routes, axis=1))
    gates = picked / jnp.sum(picked, axis=1, keepdims=True)
    batch_rows = routes.shape[0]
    topk = routes.shape[1]
    experts_all = router_weight.shape[1]
    capacity = max(2, 2 * batch_rows * topk // experts_all)
    flat_routes = routes.reshape(batch_rows * topk)
    onehot = (flat_routes[:, None] == jnp.arange(experts_all, dtype=jnp.int32)[None, :]).astype(
        jnp.int32
    )
    ranks = jnp.sum(onehot * (jnp.cumsum(onehot, axis=0) - 1), axis=1)
    target = flat_routes * capacity + ranks
    selector = (
        target[None, :] == jnp.arange(experts_all * capacity, dtype=jnp.int32)[:, None]
    ).astype(jnp.int32)
    selector = jnp.sum(selector.reshape(experts_all * capacity, batch_rows, topk), axis=2).astype(
        jnp.bfloat16
    )
    outgoing = jnp.dot(selector, normed, preferred_element_type=jnp.float32).astype(jnp.bfloat16)
    outgoing = outgoing.reshape(experts_all, capacity, width)
    received = lax.all_to_all(outgoing, ("grp", "dev"), split_axis=0, concat_axis=0, tiled=True)
    count = received.shape[0] * received.shape[1]
    gate_up = jnp.dot(
        received.reshape(count, width), expert_gate_up[0], preferred_element_type=jnp.float32
    )
    active = (jax.nn.silu(gate_up[:, :FF]) * gate_up[:, FF:]).astype(jnp.bfloat16)
    result = jnp.dot(active, expert_down[0], preferred_element_type=jnp.float32).astype(
        jnp.bfloat16
    )
    returned = lax.all_to_all(
        result.reshape(received.shape), ("grp", "dev"), split_axis=0, concat_axis=0, tiled=True
    )
    table = returned.reshape(experts_all * capacity, width)
    gathered = table[target].reshape(batch_rows, topk, width).astype(jnp.float32)
    combined = jnp.sum(gates[:, :, None] * gathered, axis=1)
    return (hidden + combined).astype(jnp.bfloat16)


def solution(mesh):
    placed = (
        P(("grp", "dev"), None),
        P(None, "dev", "grp"),
        P(None, "dev", "grp", None),
        P(None, "dev", "grp", None, None),
        P(None, "dev"),
        P("grp", None),
        P(),
        P(),
        P(("grp", "dev"), None),
        P(("grp", "dev"), None, None),
        P(("grp", "dev"), None, None),
    )
    return jax.shard_map(
        per_device, mesh=mesh, in_specs=placed, out_specs=P(("grp", "dev"), None), check_vma=False
    )
```

```python
import functools
import math

import jax
import jax.numpy as jnp
from jax import lax
from jax.experimental import pallas as pl
from jax.experimental.pallas import tpu as pltpu
from jax.sharding import PartitionSpec as P

HEAD_SIZE = 128
LANES = 128
FF = 768
CAP = 2
W_CHUNKS = 4
UNROLL = 4
VMEM_LIMIT = 48 * 1024 * 1024

F32 = jnp.float32
BF16 = jnp.bfloat16


def dot(a, b, contract=((1,), (0,))):
    return lax.dot_general(a, b, (contract, ((), ())), preferred_element_type=F32)


def attend_kernel(
    place_ref,
    length_ref,
    query_ref,
    fresh_ref,
    routes_ref,
    cache_hbm,
    weight_hbm,
    own_ref,
    other_ref,
    target_ref,
    cache_buf,
    weight_buf,
    query_buf,
    fresh_buf,
    mixed_buf,
    cache_sem,
    weight_sem,
):
    rows, kv_heads, positions, _ = cache_buf.shape
    q_heads = query_ref.shape[1] // HEAD_SIZE
    group = q_heads // kv_heads
    width = weight_buf.shape[1]
    span = width // W_CHUNKS
    scale = 1.0 / math.sqrt(HEAD_SIZE)

    def cache_copy(row):
        return pltpu.make_async_copy(cache_hbm.at[row], cache_buf.at[row], cache_sem.at[row])

    def weight_copy(part):
        cols = pl.ds(part * span, span)
        return pltpu.make_async_copy(
            weight_hbm.at[:, cols], weight_buf.at[:, cols], weight_sem.at[part]
        )

    for row in range(rows):
        cache_copy(row).start()
    for part in range(W_CHUNKS):
        weight_copy(part).start()

    routes = routes_ref[...]
    batch, topk = routes.shape
    lane = lax.broadcasted_iota(jnp.int32, (batch, LANES), 1)
    named = jnp.zeros((batch, LANES), F32)
    for k in range(topk):
        named += jnp.where(lane == routes[:, k : k + 1], 1.0, 0.0)
    below = lax.broadcasted_iota(jnp.int32, (batch, batch), 0) > lax.broadcasted_iota(
        jnp.int32, (batch, batch), 1
    )
    earlier = dot(jnp.where(below, 1.0, 0.0).astype(BF16), named.astype(BF16))
    slot = lane.astype(F32) * CAP + earlier
    target = jnp.zeros((batch, LANES), F32)
    for k in range(topk):
        found = jnp.sum(
            jnp.where(lane == routes[:, k : k + 1], slot, 0.0), axis=1, keepdims=True
        )
        target = jnp.where(lane == k, found, target)
    target_ref[...] = target.astype(jnp.int32)

    for j in range(q_heads):
        query_buf[pl.ds(j, rows, stride=q_heads), :] = query_ref[
            :, j * HEAD_SIZE : (j + 1) * HEAD_SIZE
        ].astype(F32)
    fresh_buf[...] = fresh_ref[...].astype(F32)

    position = lax.broadcasted_iota(jnp.int32, (q_heads, positions), 1)

    def one_row(row):
        first = pl.multiple_of(row * q_heads, q_heads)
        query = query_buf[pl.ds(first, q_heads), :]
        query16 = query.astype(BF16)
        fresh = fresh_buf[row]
        scores, new_key, new_value = [], [], []
        for head in range(kv_heads):
            part = dot(query16, cache_buf[row, head, :, :HEAD_SIZE], ((1,), (1,)))
            scores.append(part[head * group : (head + 1) * group])
            new_key.append(
                jnp.broadcast_to(fresh[head : head + 1, :HEAD_SIZE], (group, HEAD_SIZE))
            )
            new_value.append(
                jnp.broadcast_to(fresh[head : head + 1, HEAD_SIZE:], (group, HEAD_SIZE))
            )
        scores = jnp.concatenate(scores, axis=0) * scale
        own = jnp.sum(query * jnp.concatenate(new_key, axis=0), axis=1, keepdims=True) * scale
        raised = jnp.where(position < length_ref[row], jnp.exp(scores), 0.0)
        own = jnp.exp(own)
        total = jnp.sum(raised, axis=1, keepdims=True) + own
        weights = (raised / total).astype(BF16)
        own_weight = (own / total).astype(BF16).astype(F32)
        mixed = []
        for head in range(kv_heads):
            part = dot(weights, cache_buf[row, head, :, HEAD_SIZE:])
            mixed.append(part[head * group : (head + 1) * group])
        mixed = jnp.concatenate(mixed, axis=0) + own_weight * jnp.concatenate(new_value, axis=0)
        mixed_buf[pl.ds(first, q_heads), :] = mixed

    def some_rows(step, carry):
        for u in range(UNROLL):
            cache_copy(step * UNROLL + u).wait()
        for u in range(UNROLL):
            one_row(step * UNROLL + u)
        return carry

    lax.fori_loop(0, rows // UNROLL, some_rows, 0)

    attended = jnp.concatenate(
        [mixed_buf[pl.ds(j, rows, stride=q_heads), :].astype(BF16) for j in range(q_heads)],
        axis=1,
    )
    first_group = place_ref[0] == 0
    for part in range(W_CHUNKS):
        weight_copy(part).wait()
        cols = slice(part * span, (part + 1) * span)
        product = dot(attended, weight_buf[:, cols])
        top, bottom = product[: rows // 2], product[rows // 2 :]
        own_ref[:, cols] = jnp.where(first_group, top, bottom)
        other_ref[:, cols] = jnp.where(first_group, bottom, top)


def attend(place, length, query, fresh, routes, cache, weight):
    rows, kv_heads, positions, pair = cache.shape
    width = weight.shape[1]
    smem = pl.BlockSpec(memory_space=pltpu.SMEM)
    vmem = pl.BlockSpec(memory_space=pltpu.VMEM)
    hbm = pl.BlockSpec(memory_space=pl.ANY)
    half = jax.ShapeDtypeStruct((rows // 2, width), F32)
    return pl.pallas_call(
        attend_kernel,
        out_shape=(half, half, jax.ShapeDtypeStruct((routes.shape[0], LANES), jnp.int32)),
        in_specs=[smem, smem, vmem, vmem, vmem, hbm, hbm],
        out_specs=(vmem, vmem, vmem),
        scratch_shapes=[
            pltpu.VMEM(cache.shape, BF16),
            pltpu.VMEM(weight.shape, BF16),
            pltpu.VMEM((rows * query.shape[1] // HEAD_SIZE, HEAD_SIZE), F32),
            pltpu.VMEM(fresh.shape, F32),
            pltpu.VMEM((rows * query.shape[1] // HEAD_SIZE, HEAD_SIZE), F32),
            pltpu.SemaphoreType.DMA((rows,)),
            pltpu.SemaphoreType.DMA((W_CHUNKS,)),
        ],
        compiler_params=pltpu.CompilerParams(vmem_limit_bytes=VMEM_LIMIT),
        name="attend",
    )(place, length, query, fresh, routes, cache, weight)


def dispatch_kernel(
    target_ref,
    own_ref,
    passed_ref,
    residual_ref,
    gain_ref,
    router_ref,
    routes_ref,
    hidden_ref,
    gates_ref,
    slots_ref,
    row_buf,
):
    batch, width = own_ref.shape
    chunks = width // LANES
    topk = routes_ref.shape[1]
    hidden = residual_ref[...].astype(F32) + (own_ref[...] + passed_ref[...])
    hidden_ref[...] = hidden
    meansq = jnp.mean(hidden * hidden, axis=1, keepdims=True)
    normed = (hidden * lax.rsqrt(meansq + 1e-06) * gain_ref[...].astype(F32)).astype(BF16)
    for j in range(chunks):
        row_buf[pl.ds(j, batch, stride=chunks), :] = normed[
            :, j * LANES : (j + 1) * LANES
        ].astype(F32)

    raised = jnp.exp(dot(normed, router_ref[...]))
    routes = routes_ref[...]
    lane = lax.broadcasted_iota(jnp.int32, (batch, LANES), 1)
    total = jnp.zeros((batch, 1), F32)
    gates = jnp.zeros((batch, LANES), F32)
    for k in range(topk):
        picked = jnp.sum(
            jnp.where(lane == routes[:, k : k + 1], raised, 0.0), axis=1, keepdims=True
        )
        total += picked
        gates = jnp.where(lane == k, picked, gates)
    gates_ref[...] = gates / total

    slots_ref[...] = jnp.zeros_like(slots_ref)
    for r in range(batch):
        row = row_buf[r * chunks : (r + 1) * chunks, :].astype(BF16)
        for k in range(topk):
            slots_ref[target_ref[r, k]] = row


def dispatch(target, own, passed, residual, gain, router, routes):
    batch, width = own.shape
    smem = pl.BlockSpec(memory_space=pltpu.SMEM)
    vmem = pl.BlockSpec(memory_space=pltpu.VMEM)
    return pl.pallas_call(
        dispatch_kernel,
        out_shape=(
            jax.ShapeDtypeStruct((batch, width), F32),
            jax.ShapeDtypeStruct((batch, LANES), F32),
            jax.ShapeDtypeStruct((router.shape[1] * CAP, width // LANES, LANES), BF16),
        ),
        in_specs=[smem] + [vmem] * 6,
        out_specs=(vmem, vmem, vmem),
        scratch_shapes=[pltpu.VMEM((batch * width // LANES, LANES), F32)],
        compiler_params=pltpu.CompilerParams(vmem_limit_bytes=VMEM_LIMIT),
        name="dispatch",
    )(target, own, passed, residual, gain, router, routes)


def expert_kernel(
    x_hbm, up_hbm, down_hbm, out_ref, x_in, up_buf, down_buf, wide, x_buf, act_buf, x_sem, up_sem, down_sem
):
    count, chunks, _ = x_in.shape
    width = chunks * LANES
    step = 256
    parts = FF // step
    span = width // W_CHUNKS
    x_copy = pltpu.make_async_copy(x_hbm, x_in, x_sem)
    x_copy.start()

    def up_copy(half, part):
        cols = pl.ds(half * FF + part * step, step)
        return pltpu.make_async_copy(
            up_hbm.at[:, cols], up_buf.at[:, cols], up_sem.at[half, part]
        )

    def down_copy(part):
        cols = pl.ds(part * span, span)
        return pltpu.make_async_copy(
            down_hbm.at[:, cols], down_buf.at[:, cols], down_sem.at[part]
        )

    for part in range(parts):
        for half in range(2):
            up_copy(half, part).start()
    for part in range(W_CHUNKS):
        down_copy(part).start()

    x_copy.wait()
    wide[...] = x_in[...].reshape(count * chunks, LANES).astype(F32)
    for j in range(chunks):
        x_buf[:, j * LANES : (j + 1) * LANES] = wide[pl.ds(j, count, stride=chunks), :].astype(
            BF16
        )
    for part in range(parts):
        up_copy(0, part).wait()
        up_copy(1, part).wait()
        gate = dot(x_buf[...], up_buf[:, part * step : (part + 1) * step])
        lift = dot(x_buf[...], up_buf[:, FF + part * step : FF + (part + 1) * step])
        act_buf[:, part * step : (part + 1) * step] = (
            gate * (1.0 / (1.0 + jnp.exp(-gate))) * lift
        ).astype(BF16)
    for part in range(W_CHUNKS):
        down_copy(part).wait()
        served = dot(act_buf[...], down_buf[:, part * span : (part + 1) * span])
        for j in range(span // LANES):
            wide[pl.ds(part * (span // LANES) + j, count, stride=chunks), :] = served[
                :, j * LANES : (j + 1) * LANES
            ]
    out_ref[...] = wide[...].astype(BF16).reshape(count, chunks, LANES)


def expert(x, up, down):
    count, chunks, _ = x.shape
    vmem = pl.BlockSpec(memory_space=pltpu.VMEM)
    hbm = pl.BlockSpec(memory_space=pl.ANY)
    return pl.pallas_call(
        expert_kernel,
        out_shape=jax.ShapeDtypeStruct(x.shape, BF16),
        in_specs=[hbm, hbm, hbm],
        out_specs=vmem,
        scratch_shapes=[
            pltpu.VMEM(x.shape, BF16),
            pltpu.VMEM(up.shape, BF16),
            pltpu.VMEM(down.shape, BF16),
            pltpu.VMEM((count * chunks, LANES), F32),
            pltpu.VMEM((count, chunks * LANES), BF16),
            pltpu.VMEM((count, FF), BF16),
            pltpu.SemaphoreType.DMA,
            pltpu.SemaphoreType.DMA((2, FF // 256)),
            pltpu.SemaphoreType.DMA((W_CHUNKS,)),
        ],
        compiler_params=pltpu.CompilerParams(vmem_limit_bytes=VMEM_LIMIT),
        name="expert",
    )(x, up, down)


def combine_kernel(target_ref, gates_ref, hidden_ref, table_ref, out_ref, row_buf, *, topk):
    batch, width = hidden_ref.shape
    chunks = width // LANES
    for r in range(batch):
        total = jnp.zeros((chunks, LANES), F32)
        for k in range(topk):
            total += gates_ref[r, k] * table_ref[target_ref[r, k]].astype(F32)
        row_buf[r * chunks : (r + 1) * chunks, :] = total
    for j in range(chunks):
        cols = slice(j * LANES, (j + 1) * LANES)
        out_ref[:, cols] = (
            hidden_ref[:, cols] + row_buf[pl.ds(j, batch, stride=chunks), :]
        ).astype(BF16)


def combine(target, gates, hidden, table, topk):
    batch, width = hidden.shape
    smem = pl.BlockSpec(memory_space=pltpu.SMEM)
    vmem = pl.BlockSpec(memory_space=pltpu.VMEM)
    return pl.pallas_call(
        functools.partial(combine_kernel, topk=topk),
        out_shape=jax.ShapeDtypeStruct((batch, width), BF16),
        in_specs=[smem, smem, vmem, vmem],
        out_specs=vmem,
        scratch_shapes=[pltpu.VMEM((batch * width // LANES, LANES), F32)],
        compiler_params=pltpu.CompilerParams(vmem_limit_bytes=VMEM_LIMIT),
        name="combine",
    )(target, gates, hidden, table)


def per_device(
    residual_in,
    queries,
    latest_key_value,
    key_value_cache,
    cache_len,
    out_weight,
    norm_gain,
    router_weight,
    routes,
    expert_gate_up,
    expert_down,
):
    rows = queries.shape[0] * queries.shape[1]
    experts = router_weight.shape[1]
    topk = routes.shape[1]
    place = lax.axis_index("grp").reshape(1)
    own, other, target = attend(
        place,
        cache_len.reshape(rows),
        queries.reshape(rows, -1),
        latest_key_value.reshape((rows,) + latest_key_value.shape[2:]),
        routes,
        key_value_cache.reshape((rows,) + key_value_cache.shape[2:]),
        out_weight,
    )
    passed = lax.ppermute(other, "grp", [(0, 1), (1, 0)])
    hidden, gates, slots = dispatch(
        target, own, passed, residual_in, norm_gain.reshape(1, -1), router_weight, routes
    )
    block = (experts, CAP * slots.shape[1], LANES)
    received = lax.all_to_all(
        slots.reshape(block), ("grp", "dev"), split_axis=0, concat_axis=0, tiled=True
    )
    served = expert(received.reshape(slots.shape), expert_gate_up[0], expert_down[0])
    returned = lax.all_to_all(
        served.reshape(block), ("grp", "dev"), split_axis=0, concat_axis=0, tiled=True
    )
    return combine(target, gates, hidden, returned.reshape(slots.shape), topk)


def solution(mesh):
    placed = (
        P(("grp", "dev"), None),
        P(None, "dev", "grp"),
        P(None, "dev", "grp", None),
        P(None, "dev", "grp", None, None),
        P(None, "dev"),
        P("grp", None),
        P(),
        P(),
        P(("grp", "dev"), None),
        P(("grp", "dev"), None, None),
        P(("grp", "dev"), None, None),
    )
    return jax.shard_map(
        per_device, mesh=mesh, in_specs=placed, out_specs=P(("grp", "dev"), None), check_vma=False
    )
```

```python
import functools
import math

import jax
import jax.numpy as jnp
from jax import lax
from jax.experimental import pallas as pl
from jax.experimental.pallas import tpu as pltpu
from jax.sharding import PartitionSpec as P

HEAD_SIZE = 128
LANES = 128
FF = 768
CAP = 2
UNROLL = 8
STEP = 256
SPAN = 512
W_CHUNKS = 4
NODMA=False
MIB = 1024 * 1024
SMALL_LIMIT = 12 * MIB
EXPERT_LIMIT = 24 * MIB

F32 = jnp.float32
BF16 = jnp.bfloat16


def dot(a, b, contract=((1,), (0,))):
    return lax.dot_general(a, b, (contract, ((), ())), preferred_element_type=F32)


def attend_kernel(
    place_ref,
    length_hbm,
    query_hbm,
    fresh_hbm,
    routes_hbm,
    cache_hbm,
    weight_hbm,
    own_ref,
    other_ref,
    coded_ref,
    cache_buf,
    weight_buf,
    query_ref,
    fresh_ref,
    routes_ref,
    length_ref,
    query_buf,
    fresh_buf,
    mixed_buf,
    cache_sem,
    weight_sem,
    small_sem,
):
    rows, kv_heads, positions, _ = cache_buf.shape
    q_heads = query_ref.shape[1] // HEAD_SIZE
    group = q_heads // kv_heads
    width = weight_buf.shape[1]
    span = width // W_CHUNKS
    half_rows = rows // 2
    scale = 1.0 / math.sqrt(HEAD_SIZE)

    def whole_copy(row):
        return pltpu.make_async_copy(cache_hbm.at[row], cache_buf.at[row], cache_sem.at[row])

    def part_copy(row):
        valid = length_ref[row // half_rows, row % half_rows]
        kept = pl.ds(0, pl.multiple_of((valid + 15) // 16 * 16, 16))
        return pltpu.make_async_copy(
            cache_hbm.at[row, :, kept], cache_buf.at[row, :, kept], cache_sem.at[row]
        )

    def weight_copy(part):
        cols = pl.ds(part * span, span)
        return pltpu.make_async_copy(
            weight_hbm.at[:, cols], weight_buf.at[:, cols], weight_sem.at[part]
        )

    length_copy = pltpu.make_async_copy(length_hbm, length_ref, small_sem.at[3])
    length_copy.start()
    small_copies = [
        pltpu.make_async_copy(source, kept, small_sem.at[i])
        for i, (source, kept) in enumerate(
            ((routes_hbm, routes_ref), (query_hbm, query_ref), (fresh_hbm, fresh_ref))
        )
    ]
    for copy in small_copies:
        copy.start()
    for row in range(UNROLL):
        whole_copy(row).start()
    for row in range(UNROLL, rows):
        cache_buf[row, :, :, HEAD_SIZE:] = jnp.zeros((kv_heads, positions, HEAD_SIZE), BF16)
    length_copy.wait()
    for row in range(UNROLL, rows):
        part_copy(row).start()

    for copy in small_copies:
        copy.wait()
    topk, batch = routes_ref.shape
    unit = lax.broadcasted_iota(jnp.int32, (topk, topk), 0) == lax.broadcasted_iota(
        jnp.int32, (topk, topk), 1
    )
    routes = dot(
        routes_ref[...].astype(BF16), jnp.where(unit, 1.0, 0.0).astype(BF16), ((0,), (0,))
    ).astype(jnp.int32)
    lane = lax.broadcasted_iota(jnp.int32, (batch, LANES), 1)
    named = jnp.zeros((batch, LANES), F32)
    for k in range(topk):
        named += jnp.where(lane == routes[:, k : k + 1], 1.0, 0.0)
    below = lax.broadcasted_iota(jnp.int32, (batch, batch), 0) > lax.broadcasted_iota(
        jnp.int32, (batch, batch), 1
    )
    earlier = dot(jnp.where(below, 1.0, 0.0).astype(BF16), named.astype(BF16))
    slot = lane.astype(F32) * CAP + earlier
    target = jnp.zeros((batch, LANES), F32)
    for k in range(topk):
        found = jnp.sum(
            jnp.where(lane == routes[:, k : k + 1], slot, 0.0), axis=1, keepdims=True
        )
        target = jnp.where(lane == k, found, target)
    coded_ref[...] = target.astype(jnp.int32) ^ 1

    for j in range(q_heads):
        query_buf[pl.ds(j, rows, stride=q_heads), :] = query_ref[
            :, j * HEAD_SIZE : (j + 1) * HEAD_SIZE
        ].astype(F32)
    fresh_buf[...] = fresh_ref[...].astype(F32)

    position = lax.broadcasted_iota(jnp.int32, (q_heads, positions), 1)

    def some_rows(step, carry):
        first = step * UNROLL
        base = pl.multiple_of(first * q_heads, UNROLL * q_heads)
        query = query_buf[pl.ds(base, UNROLL * q_heads), :]
        query16 = query.astype(BF16)
        @pl.when(step == 0)
        def _():
            for u in range(UNROLL):
                whole_copy(u).wait()
            for part in range(W_CHUNKS):
                weight_copy(part).start()

        @pl.when(step > 0)
        def _():
            for u in range(UNROLL):
                part_copy(first + u).wait()

        scores, visible, new_key, new_value = [], [], [], []
        for u in range(UNROLL):
            fresh = fresh_buf[first + u]
            visible.append(position < length_ref[(first + u) // half_rows, (first + u) % half_rows])
            for head in range(kv_heads):
                begin = u * q_heads + head * group
                keys = cache_buf[first + u, head, :, :HEAD_SIZE]
                scores.append(dot(query16[begin : begin + group], keys, ((1,), (1,))))
                pair = jnp.broadcast_to(fresh[head : head + 1], (group, 2 * HEAD_SIZE))
                new_key.append(pair[:, :HEAD_SIZE])
                new_value.append(pair[:, HEAD_SIZE:])
        scores = jnp.concatenate(scores, axis=0) * scale
        new_key = jnp.concatenate(new_key, axis=0)
        own = jnp.exp(jnp.sum(query * new_key, axis=1, keepdims=True) * scale)
        raised = jnp.where(jnp.concatenate(visible, axis=0), jnp.exp(scores), 0.0)
        total = jnp.sum(raised, axis=1, keepdims=True) + own
        weights = (raised / total).astype(BF16)
        own_weight = (own / total).astype(BF16).astype(F32)
        mixed = []
        for u in range(UNROLL):
            for head in range(kv_heads):
                begin = u * q_heads + head * group
                values = cache_buf[first + u, head, :, HEAD_SIZE:]
                mixed.append(dot(weights[begin : begin + group], values))
        mixed = jnp.concatenate(mixed, axis=0) + own_weight * jnp.concatenate(new_value, axis=0)
        mixed_buf[pl.ds(base, UNROLL * q_heads), :] = mixed
        return carry

    lax.fori_loop(0, rows // UNROLL, some_rows, 0)

    attended = jnp.concatenate(
        [mixed_buf[pl.ds(j, rows, stride=q_heads), :].astype(BF16) for j in range(q_heads)],
        axis=1,
    )
    first_group = place_ref[0] == 0
    for part in range(W_CHUNKS):
        weight_copy(part).wait()
        cols = slice(part * span, (part + 1) * span)
        product = dot(attended, weight_buf[:, cols])
        top, bottom = product[: rows // 2], product[rows // 2 :]
        own_ref[:, cols] = jnp.where(first_group, top, bottom)
        other_ref[:, cols] = jnp.where(first_group, bottom, top)


def attend(place, length, query, fresh, routes, cache, weight):
    rows, kv_heads, positions, pair = cache.shape
    width = weight.shape[1]
    smem = pl.BlockSpec(memory_space=pltpu.SMEM)
    vmem = pl.BlockSpec(memory_space=pltpu.VMEM)
    hbm = pl.BlockSpec(memory_space=pltpu.HBM)
    half = jax.ShapeDtypeStruct((rows // 2, width), F32)
    return pl.pallas_call(
        attend_kernel,
        out_shape=(half, half, jax.ShapeDtypeStruct((routes.shape[1], LANES), jnp.int32)),
        in_specs=[smem, hbm, hbm, hbm, hbm, hbm, hbm],
        out_specs=(vmem, vmem, vmem),
        scratch_shapes=[
            pltpu.VMEM(cache.shape, BF16),
            pltpu.VMEM(weight.shape, BF16),
            pltpu.VMEM(query.shape, BF16),
            pltpu.VMEM(fresh.shape, BF16),
            pltpu.VMEM(routes.shape, jnp.int32),
            pltpu.SMEM(length.shape, jnp.int32),
            pltpu.VMEM((rows * query.shape[1] // HEAD_SIZE, HEAD_SIZE), F32),
            pltpu.VMEM(fresh.shape, F32),
            pltpu.VMEM((rows * query.shape[1] // HEAD_SIZE, HEAD_SIZE), F32),
            pltpu.SemaphoreType.DMA((rows,)),
            pltpu.SemaphoreType.DMA((W_CHUNKS,)),
            pltpu.SemaphoreType.DMA((4,)),
        ],
        compiler_params=pltpu.CompilerParams(vmem_limit_bytes=63 * MIB),
        name="attend",
    )(place, length, query, fresh, routes, cache, weight)


def dispatch_kernel(
    target_ref,
    named_ref,
    base_ref,
    passed_ref,
    gain_ref,
    router_ref,
    hidden_ref,
    gates_ref,
    slots_ref,
    row_buf,
    *,
    topk,
):
    batch, width = base_ref.shape
    chunks = width // LANES
    hidden = base_ref[...] + passed_ref[...]
    hidden_ref[...] = hidden
    meansq = jnp.mean(hidden * hidden, axis=1, keepdims=True)
    normed = (hidden * lax.rsqrt(meansq + 1e-06) * gain_ref[...].astype(F32)).astype(BF16)
    for j in range(chunks):
        row_buf[pl.ds(j, batch, stride=chunks), :] = normed[
            :, j * LANES : (j + 1) * LANES
        ].astype(F32)

    raised = jnp.exp(dot(normed, router_ref[...]))
    routes = named_ref[...]
    lane = lax.broadcasted_iota(jnp.int32, (batch, LANES), 1)
    total = jnp.zeros((batch, 1), F32)
    gates = jnp.zeros((batch, LANES), F32)
    for k in range(topk):
        picked = jnp.sum(
            jnp.where(lane == routes[:, k : k + 1], raised, 0.0), axis=1, keepdims=True
        )
        total += picked
        gates = jnp.where(lane == k, picked, gates)
    gates_ref[...] = gates / total

    slots_ref[...] = jnp.zeros_like(slots_ref)
    for r in range(batch):
        row = row_buf[r * chunks : (r + 1) * chunks, :].astype(BF16)
        for k in range(topk):
            slots_ref[target_ref[r, k]] = row


def dispatch(target, named, base, passed, gain, router, topk):
    batch, width = base.shape
    smem = pl.BlockSpec(memory_space=pltpu.SMEM)
    vmem = pl.BlockSpec(memory_space=pltpu.VMEM)
    return pl.pallas_call(
        functools.partial(dispatch_kernel, topk=topk),
        out_shape=(
            jax.ShapeDtypeStruct((batch, width), F32),
            jax.ShapeDtypeStruct((batch, LANES), F32),
            jax.ShapeDtypeStruct((router.shape[1] * CAP, width // LANES, LANES), BF16),
        ),
        in_specs=[smem] + [vmem] * 5,
        out_specs=(vmem, vmem, vmem),
        scratch_shapes=[pltpu.VMEM((batch * width // LANES, LANES), F32)],
        compiler_params=pltpu.CompilerParams(vmem_limit_bytes=SMALL_LIMIT),
        cost_estimate=pl.CostEstimate(
            flops=10_000_000_000, bytes_accessed=3_000_000, transcendentals=0
        ),
        name="dispatch",
    )(target, named, base, passed, gain, router)


def expert_kernel(x_ref, up_ref, down_ref, out_ref, wide, x_buf, act_buf):
    count, chunks, _ = x_ref.shape
    width = chunks * LANES
    step = STEP
    span = SPAN
    wide[...] = x_ref[...].reshape(count * chunks, LANES).astype(F32)
    for j in range(chunks):
        x_buf[:, j * LANES : (j + 1) * LANES] = wide[pl.ds(j, count, stride=chunks), :].astype(
            BF16
        )
    for part in range(FF // step):
        gate = dot(x_buf[...], up_ref[:, part * step : (part + 1) * step])
        lift = dot(x_buf[...], up_ref[:, FF + part * step : FF + (part + 1) * step])
        act_buf[:, part * step : (part + 1) * step] = (
            gate * (1.0 / (1.0 + jnp.exp(-gate))) * lift
        ).astype(BF16)
    for part in range(width // span):
        served = dot(act_buf[...], down_ref[:, part * span : (part + 1) * span])
        for j in range(span // LANES):
            wide[pl.ds(part * (span // LANES) + j, count, stride=chunks), :] = served[
                :, j * LANES : (j + 1) * LANES
            ]
    out_ref[...] = wide[...].astype(BF16).reshape(count, chunks, LANES)


def expert(x, up, down):
    count, chunks, _ = x.shape
    vmem = pl.BlockSpec(memory_space=pltpu.VMEM)
    return pl.pallas_call(
        expert_kernel,
        out_shape=jax.ShapeDtypeStruct(x.shape, BF16),
        in_specs=[vmem, vmem, vmem],
        out_specs=vmem,
        scratch_shapes=[
            pltpu.VMEM((count * chunks, LANES), F32),
            pltpu.VMEM((count, chunks * LANES), BF16),
            pltpu.VMEM((count, FF), BF16),
        ],
        compiler_params=pltpu.CompilerParams(vmem_limit_bytes=EXPERT_LIMIT),
        name="expert",
    )(x, up, down)


def combine_kernel(target_ref, gates_ref, hidden_ref, table_ref, out_ref, row_buf, *, topk):
    batch, width = hidden_ref.shape
    chunks = width // LANES
    for r in range(batch):
        total = jnp.zeros((chunks, LANES), F32)
        for k in range(topk):
            total += gates_ref[r, k] * table_ref[target_ref[r, k]].astype(F32)
        row_buf[r * chunks : (r + 1) * chunks, :] = total
    for j in range(chunks):
        cols = slice(j * LANES, (j + 1) * LANES)
        out_ref[:, cols] = (
            hidden_ref[:, cols] + row_buf[pl.ds(j, batch, stride=chunks), :]
        ).astype(BF16)


def combine(target, gates, hidden, table, topk):
    batch, width = hidden.shape
    smem = pl.BlockSpec(memory_space=pltpu.SMEM)
    vmem = pl.BlockSpec(memory_space=pltpu.VMEM)
    return pl.pallas_call(
        functools.partial(combine_kernel, topk=topk),
        out_shape=jax.ShapeDtypeStruct((batch, width), BF16),
        in_specs=[smem, smem, vmem, vmem],
        out_specs=vmem,
        scratch_shapes=[pltpu.VMEM((batch * width // LANES, LANES), F32)],
        compiler_params=pltpu.CompilerParams(vmem_limit_bytes=SMALL_LIMIT),
        name="combine",
    )(target, gates, hidden, table)


def per_device(
    residual_in,
    queries,
    latest_key_value,
    key_value_cache,
    cache_len,
    out_weight,
    norm_gain,
    router_weight,
    routes,
    expert_gate_up,
    expert_down,
):
    rows = queries.shape[0] * queries.shape[1]
    experts = router_weight.shape[1]
    topk = routes.shape[1]
    place = lax.axis_index("grp").reshape(1)
    own, other, coded = attend(
        place,
        cache_len,
        queries.reshape(rows, -1),
        latest_key_value.reshape((rows,) + latest_key_value.shape[2:]),
        routes.T,
        key_value_cache.reshape((rows,) + key_value_cache.shape[2:]),
        out_weight,
    )
    passed = lax.ppermute(other, "grp", [(0, 1), (1, 0)])
    base = residual_in.astype(F32) + own
    named, target = coded >> 1, coded ^ 1
    hidden, gates, slots = dispatch(
        target, named, base, passed, norm_gain.reshape(1, -1), router_weight, topk
    )
    block = (experts, CAP * slots.shape[1], LANES)
    received = lax.all_to_all(
        slots.reshape(block), ("grp", "dev"), split_axis=0, concat_axis=0, tiled=True
    )
    served = expert(received.reshape(slots.shape), expert_gate_up[0], expert_down[0])
    returned = lax.all_to_all(
        served.reshape(block), ("grp", "dev"), split_axis=0, concat_axis=0, tiled=True
    )
    return combine(target, gates, hidden, returned.reshape(slots.shape), topk)


def solution(mesh):
    placed = (
        P(("grp", "dev"), None),
        P(None, "dev", "grp"),
        P(None, "dev", "grp", None),
        P(None, "dev", "grp", None, None),
        P(None, "dev"),
        P("grp", None),
        P(),
        P(),
        P(("grp", "dev"), None),
        P(("grp", "dev"), None, None),
        P(("grp", "dev"), None, None),
    )
    return jax.shard_map(
        per_device, mesh=mesh, in_specs=placed, out_specs=P(("grp", "dev"), None), check_vma=False
    )
```

```python
import functools
import math

import jax
import jax.numpy as jnp
from jax import lax
from jax.experimental import pallas as pl
from jax.experimental.pallas import tpu as pltpu
from jax.sharding import PartitionSpec as P

HEAD_SIZE = 128
LANES = 128
FF = 768
CAP = 2
UNROLL = 8
WHOLE = 8
WSTEP = 0
TSTEP = 0
STEP = 256
SPAN = 512
W_CHUNKS = 4
NODMA=False
MIB = 1024 * 1024
SMALL_LIMIT = 12 * MIB
EXPERT_LIMIT = 24 * MIB

F32 = jnp.float32
BF16 = jnp.bfloat16


def dot(a, b, contract=((1,), (0,))):
    return lax.dot_general(a, b, (contract, ((), ())), preferred_element_type=F32)


def attend_kernel(
    place_ref,
    length_hbm,
    query_hbm,
    fresh_hbm,
    routes_hbm,
    cache_hbm,
    weight_hbm,
    own_ref,
    other_ref,
    cache_buf,
    weight_buf,
    query_ref,
    fresh_ref,
    routes_ref,
    length_ref,
    query_buf,
    fresh_buf,
    mixed_buf,
    cache_sem,
    weight_sem,
    small_sem,
):
    rows, kv_heads, positions, _ = cache_buf.shape
    q_heads = query_ref.shape[1] // HEAD_SIZE
    group = q_heads // kv_heads
    width = weight_buf.shape[1]
    span = width // W_CHUNKS
    half_rows = rows // 2
    scale = 1.0 / math.sqrt(HEAD_SIZE)

    def whole_copy(row):
        return pltpu.make_async_copy(cache_hbm.at[row], cache_buf.at[row], cache_sem.at[row])

    def part_copy(row):
        valid = length_ref[row // half_rows, row % half_rows]
        kept = pl.ds(0, pl.multiple_of((valid + 15) // 16 * 16, 16))
        return pltpu.make_async_copy(
            cache_hbm.at[row, :, kept], cache_buf.at[row, :, kept], cache_sem.at[row]
        )

    def weight_copy(part):
        cols = pl.ds(part * span, span)
        return pltpu.make_async_copy(
            weight_hbm.at[:, cols], weight_buf.at[:, cols], weight_sem.at[part]
        )

    length_copy = pltpu.make_async_copy(length_hbm, length_ref, small_sem.at[3])
    length_copy.start()
    small_copies = [
        pltpu.make_async_copy(source, kept, small_sem.at[i])
        for i, (source, kept) in enumerate(
            ((routes_hbm, routes_ref), (query_hbm, query_ref), (fresh_hbm, fresh_ref))
        )
    ]
    for copy in small_copies:
        copy.start()
    for row in range(WHOLE):
        whole_copy(row).start()
    for row in range(WHOLE, rows):
        cache_buf[row, :, :, HEAD_SIZE:] = jnp.zeros((kv_heads, positions, HEAD_SIZE), BF16)
    length_copy.wait()
    for row in range(WHOLE, rows):
        part_copy(row).start()

    for copy in small_copies:
        copy.wait()
    for j in range(q_heads):
        query_buf[pl.ds(j, rows, stride=q_heads), :] = query_ref[
            :, j * HEAD_SIZE : (j + 1) * HEAD_SIZE
        ].astype(F32)
    fresh_buf[...] = fresh_ref[...].astype(F32)

    def place_rows():
        topk, batch = routes_ref.shape
        unit = lax.broadcasted_iota(jnp.int32, (topk, topk), 0) == lax.broadcasted_iota(
            jnp.int32, (topk, topk), 1
        )
        routes = dot(
            routes_ref[...].astype(BF16), jnp.where(unit, 1.0, 0.0).astype(BF16), ((0,), (0,))
        ).astype(jnp.int32)
        lane = lax.broadcasted_iota(jnp.int32, (batch, LANES), 1)
        named = jnp.zeros((batch, LANES), F32)
        for k in range(topk):
            named += jnp.where(lane == routes[:, k : k + 1], 1.0, 0.0)
        below = lax.broadcasted_iota(jnp.int32, (batch, batch), 0) > lax.broadcasted_iota(
            jnp.int32, (batch, batch), 1
        )
        earlier = dot(jnp.where(below, 1.0, 0.0).astype(BF16), named.astype(BF16))
        slot = lane.astype(F32) * CAP + earlier
        target = jnp.zeros((batch, LANES), F32)
        for k in range(topk):
            found = jnp.sum(
                jnp.where(lane == routes[:, k : k + 1], slot, 0.0), axis=1, keepdims=True
            )
            target = jnp.where(lane == k, found, target)
        own_ref[batch:, :LANES] = target[: batch // 2]
        own_ref[batch:, LANES : 2 * LANES] = target[batch // 2 :]
        own_ref[batch:, 2 * LANES :] = jnp.zeros((batch // 2, width - 2 * LANES), F32)

    position = lax.broadcasted_iota(jnp.int32, (q_heads, positions), 1)

    def score(step):
        first = step * UNROLL
        query = query_buf[first * q_heads : (first + UNROLL) * q_heads, :]
        query16 = query.astype(BF16)
        scores, visible, new_key, new_value = [], [], [], []
        for u in range(UNROLL):
            fresh = fresh_buf[first + u]
            valid = length_ref[(first + u) // half_rows, (first + u) % half_rows]
            visible.append(position < valid)
            for head in range(kv_heads):
                begin = u * q_heads + head * group
                keys = cache_buf[first + u, head, :, :HEAD_SIZE]
                scores.append(dot(query16[begin : begin + group], keys, ((1,), (1,))))
                pair = jnp.broadcast_to(fresh[head : head + 1], (group, 2 * HEAD_SIZE))
                new_key.append(pair[:, :HEAD_SIZE])
                new_value.append(pair[:, HEAD_SIZE:])
        scores = jnp.concatenate(scores, axis=0) * scale
        new_key = jnp.concatenate(new_key, axis=0)
        own = jnp.exp(jnp.sum(query * new_key, axis=1, keepdims=True) * scale)
        raised = jnp.where(jnp.concatenate(visible, axis=0), jnp.exp(scores), 0.0)
        return raised, own, jnp.concatenate(new_value, axis=0)

    def mix(step, raised, own, new_value):
        first = step * UNROLL
        total = jnp.sum(raised, axis=1, keepdims=True) + own
        weights = (raised / total).astype(BF16)
        own_weight = (own / total).astype(BF16).astype(F32)
        mixed = []
        for u in range(UNROLL):
            for head in range(kv_heads):
                begin = u * q_heads + head * group
                values = cache_buf[first + u, head, :, HEAD_SIZE:]
                mixed.append(dot(weights[begin : begin + group], values))
        mixed = jnp.concatenate(mixed, axis=0) + own_weight * new_value
        mixed_buf[first * q_heads : (first + UNROLL) * q_heads, :] = mixed

    ready = None
    for step in range(rows // UNROLL):
        for u in range(UNROLL):
            row = step * UNROLL + u
            (whole_copy if row < WHOLE else part_copy)(row).wait()
        if step == WSTEP:
            for part in range(W_CHUNKS):
                weight_copy(part).start()
        if step == TSTEP:
            place_rows()
        scored = score(step)
        if step:
            mix(step - 1, *ready)
        ready = scored
    mix(step, *ready)

    attended = jnp.concatenate(
        [mixed_buf[pl.ds(j, rows, stride=q_heads), :].astype(BF16) for j in range(q_heads)],
        axis=1,
    )
    first_group = place_ref[0] == 0
    for part in range(W_CHUNKS):
        weight_copy(part).wait()
        cols = slice(part * span, (part + 1) * span)
        product = dot(attended, weight_buf[:, cols])
        top, bottom = product[: rows // 2], product[rows // 2 :]
        own_ref[:half_rows, cols] = jnp.where(first_group, top, bottom)
        other_ref[:, cols] = jnp.where(first_group, bottom, top)


def attend(place, length, query, fresh, routes, cache, weight):
    rows, kv_heads, positions, pair = cache.shape
    width = weight.shape[1]
    smem = pl.BlockSpec(memory_space=pltpu.SMEM)
    vmem = pl.BlockSpec(memory_space=pltpu.VMEM)
    hbm = pl.BlockSpec(memory_space=pltpu.HBM)
    half = rows // 2
    return pl.pallas_call(
        attend_kernel,
        out_shape=(
            jax.ShapeDtypeStruct((half + half // 2, width), F32),
            jax.ShapeDtypeStruct((half, width), F32),
        ),
        in_specs=[smem, hbm, hbm, hbm, hbm, hbm, hbm],
        out_specs=(vmem, vmem),
        scratch_shapes=[
            pltpu.VMEM(cache.shape, BF16),
            pltpu.VMEM(weight.shape, BF16),
            pltpu.VMEM(query.shape, BF16),
            pltpu.VMEM(fresh.shape, BF16),
            pltpu.VMEM(routes.shape, jnp.int32),
            pltpu.SMEM(length.shape, jnp.int32),
            pltpu.VMEM((rows * query.shape[1] // HEAD_SIZE, HEAD_SIZE), F32),
            pltpu.VMEM(fresh.shape, F32),
            pltpu.VMEM((rows * query.shape[1] // HEAD_SIZE, HEAD_SIZE), F32),
            pltpu.SemaphoreType.DMA((rows,)),
            pltpu.SemaphoreType.DMA((W_CHUNKS,)),
            pltpu.SemaphoreType.DMA((4,)),
        ],
        compiler_params=pltpu.CompilerParams(vmem_limit_bytes=63 * MIB),
        name="attend",
    )(place, length, query, fresh, routes, cache, weight)


def dispatch_kernel(
    base_ref,
    passed_ref,
    gain_ref,
    router_ref,
    hidden_ref,
    target_ref,
    gates_ref,
    slots_ref,
    row_buf,
    place_ref,
    place_sem,
    *,
    topk,
):
    batch, width = passed_ref.shape
    chunks = width // LANES
    target = jnp.concatenate(
        [base_ref[batch:, :LANES], base_ref[batch:, LANES : 2 * LANES]], axis=0
    ).astype(jnp.int32)
    target_ref[...] = target
    place_copy = pltpu.make_async_copy(target_ref, place_ref, place_sem)
    place_copy.start()
    hidden = base_ref[:batch, :] + passed_ref[...]
    hidden_ref[...] = hidden
    meansq = jnp.mean(hidden * hidden, axis=1, keepdims=True)
    normed = (hidden * lax.rsqrt(meansq + 1e-06) * gain_ref[...].astype(F32)).astype(BF16)
    for j in range(chunks):
        row_buf[pl.ds(j, batch, stride=chunks), :] = normed[
            :, j * LANES : (j + 1) * LANES
        ].astype(F32)

    raised = jnp.exp(dot(normed, router_ref[...]))
    routes = target // CAP
    lane = lax.broadcasted_iota(jnp.int32, (batch, LANES), 1)
    total = jnp.zeros((batch, 1), F32)
    gates = jnp.zeros((batch, LANES), F32)
    for k in range(topk):
        picked = jnp.sum(
            jnp.where(lane == routes[:, k : k + 1], raised, 0.0), axis=1, keepdims=True
        )
        total += picked
        gates = jnp.where(lane == k, picked, gates)
    gates_ref[...] = gates / total

    slots_ref[...] = jnp.zeros_like(slots_ref)
    place_copy.wait()
    for r in range(batch):
        row = row_buf[r * chunks : (r + 1) * chunks, :].astype(BF16)
        for k in range(topk):
            slots_ref[place_ref[r, k]] = row


def dispatch(base, passed, gain, router, topk):
    batch, width = passed.shape
    vmem = pl.BlockSpec(memory_space=pltpu.VMEM)
    return pl.pallas_call(
        functools.partial(dispatch_kernel, topk=topk),
        out_shape=(
            jax.ShapeDtypeStruct((batch, width), F32),
            jax.ShapeDtypeStruct((batch, LANES), jnp.int32),
            jax.ShapeDtypeStruct((batch, LANES), F32),
            jax.ShapeDtypeStruct((router.shape[1] * CAP, width // LANES, LANES), BF16),
        ),
        in_specs=[vmem] * 4,
        out_specs=(vmem, vmem, vmem, vmem),
        scratch_shapes=[
            pltpu.VMEM((batch * width // LANES, LANES), F32),
            pltpu.SMEM((batch, LANES), jnp.int32),
            pltpu.SemaphoreType.DMA,
        ],
        compiler_params=pltpu.CompilerParams(vmem_limit_bytes=SMALL_LIMIT),
        cost_estimate=pl.CostEstimate(
            flops=10_000_000_000, bytes_accessed=3_000_000, transcendentals=0
        ),
        name="dispatch",
    )(base, passed, gain, router)


def expert_kernel(x_ref, up_ref, down_ref, out_ref, wide, x_buf, act_buf):
    count, chunks, _ = x_ref.shape
    width = chunks * LANES
    step = STEP
    span = SPAN
    wide[...] = x_ref[...].reshape(count * chunks, LANES).astype(F32)
    for j in range(chunks):
        x_buf[:, j * LANES : (j + 1) * LANES] = wide[pl.ds(j, count, stride=chunks), :].astype(
            BF16
        )
    for part in range(FF // step):
        gate = dot(x_buf[...], up_ref[:, part * step : (part + 1) * step])
        lift = dot(x_buf[...], up_ref[:, FF + part * step : FF + (part + 1) * step])
        act_buf[:, part * step : (part + 1) * step] = (
            gate * (1.0 / (1.0 + jnp.exp(-gate))) * lift
        ).astype(BF16)
    for part in range(width // span):
        served = dot(act_buf[...], down_ref[:, part * span : (part + 1) * span])
        for j in range(span // LANES):
            wide[pl.ds(part * (span // LANES) + j, count, stride=chunks), :] = served[
                :, j * LANES : (j + 1) * LANES
            ]
    out_ref[...] = wide[...].astype(BF16).reshape(count, chunks, LANES)


def expert(x, up, down):
    count, chunks, _ = x.shape
    vmem = pl.BlockSpec(memory_space=pltpu.VMEM)
    return pl.pallas_call(
        expert_kernel,
        out_shape=jax.ShapeDtypeStruct(x.shape, BF16),
        in_specs=[vmem, vmem, vmem],
        out_specs=vmem,
        scratch_shapes=[
            pltpu.VMEM((count * chunks, LANES), F32),
            pltpu.VMEM((count, chunks * LANES), BF16),
            pltpu.VMEM((count, FF), BF16),
        ],
        compiler_params=pltpu.CompilerParams(vmem_limit_bytes=EXPERT_LIMIT),
        name="expert",
    )(x, up, down)


def combine_kernel(target_ref, gates_ref, hidden_ref, table_ref, out_ref, row_buf, *, topk):
    batch, width = hidden_ref.shape
    chunks = width // LANES
    for r in range(batch):
        total = jnp.zeros((chunks, LANES), F32)
        for k in range(topk):
            total += gates_ref[r, k] * table_ref[target_ref[r, k]].astype(F32)
        row_buf[r * chunks : (r + 1) * chunks, :] = total
    for j in range(chunks):
        cols = slice(j * LANES, (j + 1) * LANES)
        out_ref[:, cols] = (
            hidden_ref[:, cols] + row_buf[pl.ds(j, batch, stride=chunks), :]
        ).astype(BF16)


def combine(target, gates, hidden, table, topk):
    batch, width = hidden.shape
    smem = pl.BlockSpec(memory_space=pltpu.SMEM)
    vmem = pl.BlockSpec(memory_space=pltpu.VMEM)
    return pl.pallas_call(
        functools.partial(combine_kernel, topk=topk),
        out_shape=jax.ShapeDtypeStruct((batch, width), BF16),
        in_specs=[smem, smem, vmem, vmem],
        out_specs=vmem,
        scratch_shapes=[pltpu.VMEM((batch * width // LANES, LANES), F32)],
        compiler_params=pltpu.CompilerParams(vmem_limit_bytes=SMALL_LIMIT),
        name="combine",
    )(target, gates, hidden, table)


def per_device(
    residual_in,
    queries,
    latest_key_value,
    key_value_cache,
    cache_len,
    out_weight,
    norm_gain,
    router_weight,
    routes,
    expert_gate_up,
    expert_down,
):
    rows = queries.shape[0] * queries.shape[1]
    experts = router_weight.shape[1]
    topk = routes.shape[1]
    place = lax.axis_index("grp").reshape(1)
    own, other = attend(
        place,
        cache_len,
        queries.reshape(rows, -1),
        latest_key_value.reshape((rows,) + latest_key_value.shape[2:]),
        routes.T,
        key_value_cache.reshape((rows,) + key_value_cache.shape[2:]),
        out_weight,
    )
    passed = lax.ppermute(other, "grp", [(0, 1), (1, 0)])
    below = own.shape[0] - residual_in.shape[0]
    base = jnp.pad(residual_in.astype(F32), ((0, below), (0, 0))) + own
    hidden, target, gates, slots = dispatch(
        base, passed, norm_gain.reshape(1, -1), router_weight, topk
    )
    block = (experts, CAP * slots.shape[1], LANES)
    received = lax.all_to_all(
        slots.reshape(block), ("grp", "dev"), split_axis=0, concat_axis=0, tiled=True
    )
    served = expert(received.reshape(slots.shape), expert_gate_up[0], expert_down[0])
    returned = lax.all_to_all(
        served.reshape(block), ("grp", "dev"), split_axis=0, concat_axis=0, tiled=True
    )
    return combine(target, gates, hidden, returned.reshape(slots.shape), topk)


def solution(mesh):
    placed = (
        P(("grp", "dev"), None),
        P(None, "dev", "grp"),
        P(None, "dev", "grp", None),
        P(None, "dev", "grp", None, None),
        P(None, "dev"),
        P("grp", None),
        P(),
        P(),
        P(("grp", "dev"), None),
        P(("grp", "dev"), None, None),
        P(("grp", "dev"), None, None),
    )
    return jax.shard_map(
        per_device, mesh=mesh, in_specs=placed, out_specs=P(("grp", "dev"), None), check_vma=False
    )
```

```python
import functools
import math

import jax
import jax.numpy as jnp
from jax import lax
from jax.experimental import pallas as pl
from jax.experimental.pallas import tpu as pltpu
from jax.sharding import PartitionSpec as P

HEAD_SIZE = 128
LANES = 128
FF = 768
CAP = 2
UNROLL = 8
WHOLE = 8
WSTEP = 0
TSTEP = 0
STEP = 256
SPAN = 512
W_CHUNKS = 4
NODMA=False
MIB = 1024 * 1024
SMALL_LIMIT = 12 * MIB
EXPERT_LIMIT = 24 * MIB

F32 = jnp.float32
BF16 = jnp.bfloat16


def dot(a, b, contract=((1,), (0,))):
    return lax.dot_general(a, b, (contract, ((), ())), preferred_element_type=F32)


def attend_kernel(
    place_ref,
    length_hbm,
    query_hbm,
    fresh_hbm,
    routes_hbm,
    cache_hbm,
    weight_hbm,
    own_ref,
    other_ref,
    cache_buf,
    weight_buf,
    query_ref,
    fresh_ref,
    routes_ref,
    length_ref,
    query_buf,
    fresh_buf,
    mixed_buf,
    cache_sem,
    weight_sem,
    small_sem,
):
    rows, kv_heads, positions, _ = cache_buf.shape
    q_heads = query_ref.shape[1] // HEAD_SIZE
    group = q_heads // kv_heads
    width = weight_buf.shape[1]
    span = width // W_CHUNKS
    half_rows = rows // 2
    scale = 1.0 / math.sqrt(HEAD_SIZE)

    def whole_copy(row):
        return pltpu.make_async_copy(cache_hbm.at[row], cache_buf.at[row], cache_sem.at[row])

    def part_copy(row):
        valid = length_ref[row // half_rows, row % half_rows]
        kept = pl.ds(0, pl.multiple_of((valid + 15) // 16 * 16, 16))
        return pltpu.make_async_copy(
            cache_hbm.at[row, :, kept], cache_buf.at[row, :, kept], cache_sem.at[row]
        )

    def weight_copy(part):
        cols = pl.ds(part * span, span)
        return pltpu.make_async_copy(
            weight_hbm.at[:, cols], weight_buf.at[:, cols], weight_sem.at[part]
        )

    length_copy = pltpu.make_async_copy(length_hbm, length_ref, small_sem.at[3])
    length_copy.start()
    small_copies = [
        pltpu.make_async_copy(source, kept, small_sem.at[i])
        for i, (source, kept) in enumerate(
            ((routes_hbm, routes_ref), (query_hbm, query_ref), (fresh_hbm, fresh_ref))
        )
    ]
    for copy in small_copies:
        copy.start()
    for row in range(WHOLE):
        whole_copy(row).start()
    for row in range(WHOLE, rows):
        cache_buf[row, :, :, HEAD_SIZE:] = jnp.zeros((kv_heads, positions, HEAD_SIZE), BF16)
    length_copy.wait()
    for row in range(WHOLE, rows):
        part_copy(row).start()

    for copy in small_copies:
        copy.wait()
    for j in range(q_heads):
        query_buf[pl.ds(j, rows, stride=q_heads), :] = query_ref[
            :, j * HEAD_SIZE : (j + 1) * HEAD_SIZE
        ].astype(F32)
    fresh_buf[...] = fresh_ref[...].astype(F32)

    def place_rows():
        topk, batch = routes_ref.shape
        unit = lax.broadcasted_iota(jnp.int32, (topk, topk), 0) == lax.broadcasted_iota(
            jnp.int32, (topk, topk), 1
        )
        routes = dot(
            routes_ref[...].astype(BF16), jnp.where(unit, 1.0, 0.0).astype(BF16), ((0,), (0,))
        ).astype(jnp.int32)
        lane = lax.broadcasted_iota(jnp.int32, (batch, LANES), 1)
        named = jnp.zeros((batch, LANES), F32)
        for k in range(topk):
            named += jnp.where(lane == routes[:, k : k + 1], 1.0, 0.0)
        below = lax.broadcasted_iota(jnp.int32, (batch, batch), 0) > lax.broadcasted_iota(
            jnp.int32, (batch, batch), 1
        )
        earlier = dot(jnp.where(below, 1.0, 0.0).astype(BF16), named.astype(BF16))
        slot = lane.astype(F32) * CAP + earlier
        target = jnp.zeros((batch, LANES), F32)
        for k in range(topk):
            found = jnp.sum(
                jnp.where(lane == routes[:, k : k + 1], slot, 0.0), axis=1, keepdims=True
            )
            target = jnp.where(lane == k, found, target)
        own_ref[batch:, :LANES] = target[: batch // 2]
        own_ref[batch:, LANES : 2 * LANES] = target[batch // 2 :]
        own_ref[batch:, 2 * LANES :] = jnp.zeros((batch // 2, width - 2 * LANES), F32)

    position = lax.broadcasted_iota(jnp.int32, (q_heads, positions), 1)

    def score(step):
        first = step * UNROLL
        query = query_buf[first * q_heads : (first + UNROLL) * q_heads, :]
        query16 = query.astype(BF16)
        scores, visible, new_key, new_value = [], [], [], []
        for u in range(UNROLL):
            fresh = fresh_buf[first + u]
            valid = length_ref[(first + u) // half_rows, (first + u) % half_rows]
            visible.append(position < valid)
            for head in range(kv_heads):
                begin = u * q_heads + head * group
                keys = cache_buf[first + u, head, :, :HEAD_SIZE]
                scores.append(dot(query16[begin : begin + group], keys, ((1,), (1,))))
                pair = jnp.broadcast_to(fresh[head : head + 1], (group, 2 * HEAD_SIZE))
                new_key.append(pair[:, :HEAD_SIZE])
                new_value.append(pair[:, HEAD_SIZE:])
        scores = jnp.concatenate(scores, axis=0) * scale
        new_key = jnp.concatenate(new_key, axis=0)
        own = jnp.exp(jnp.sum(query * new_key, axis=1, keepdims=True) * scale)
        raised = jnp.where(jnp.concatenate(visible, axis=0), jnp.exp(scores), 0.0)
        return raised, own, jnp.concatenate(new_value, axis=0)

    def mix(step, raised, own, new_value):
        first = step * UNROLL
        total = jnp.sum(raised, axis=1, keepdims=True) + own
        weights = (raised / total).astype(BF16)
        own_weight = (own / total).astype(BF16).astype(F32)
        mixed = []
        for u in range(UNROLL):
            for head in range(kv_heads):
                begin = u * q_heads + head * group
                values = cache_buf[first + u, head, :, HEAD_SIZE:]
                mixed.append(dot(weights[begin : begin + group], values))
        mixed = jnp.concatenate(mixed, axis=0) + own_weight * new_value
        mixed_buf[first * q_heads : (first + UNROLL) * q_heads, :] = mixed

    ready = None
    for step in range(rows // UNROLL):
        for u in range(UNROLL):
            row = step * UNROLL + u
            (whole_copy if row < WHOLE else part_copy)(row).wait()
        if step == WSTEP:
            for part in range(W_CHUNKS):
                weight_copy(part).start()
        if step == TSTEP:
            place_rows()
        scored = score(step)
        if step:
            mix(step - 1, *ready)
        ready = scored
    mix(step, *ready)

    attended = jnp.concatenate(
        [mixed_buf[pl.ds(j, rows, stride=q_heads), :].astype(BF16) for j in range(q_heads)],
        axis=1,
    )
    first_group = place_ref[0] == 0
    for part in range(W_CHUNKS):
        weight_copy(part).wait()
        cols = slice(part * span, (part + 1) * span)
        product = dot(attended, weight_buf[:, cols])
        top, bottom = product[: rows // 2], product[rows // 2 :]
        own_ref[:half_rows, cols] = jnp.where(first_group, top, bottom)
        other_ref[:, cols] = jnp.where(first_group, bottom, top)


def attend(place, length, query, fresh, routes, cache, weight):
    rows, kv_heads, positions, pair = cache.shape
    width = weight.shape[1]
    smem = pl.BlockSpec(memory_space=pltpu.SMEM)
    vmem = pl.BlockSpec(memory_space=pltpu.VMEM)
    hbm = pl.BlockSpec(memory_space=pltpu.HBM)
    half = rows // 2
    return pl.pallas_call(
        attend_kernel,
        out_shape=(
            jax.ShapeDtypeStruct((half + half // 2, width), F32),
            jax.ShapeDtypeStruct((half, width), F32),
        ),
        in_specs=[smem, hbm, hbm, hbm, hbm, hbm, hbm],
        out_specs=(vmem, vmem),
        scratch_shapes=[
            pltpu.VMEM(cache.shape, BF16),
            pltpu.VMEM(weight.shape, BF16),
            pltpu.VMEM(query.shape, BF16),
            pltpu.VMEM(fresh.shape, BF16),
            pltpu.VMEM(routes.shape, jnp.int32),
            pltpu.SMEM(length.shape, jnp.int32),
            pltpu.VMEM((rows * query.shape[1] // HEAD_SIZE, HEAD_SIZE), F32),
            pltpu.VMEM(fresh.shape, F32),
            pltpu.VMEM((rows * query.shape[1] // HEAD_SIZE, HEAD_SIZE), F32),
            pltpu.SemaphoreType.DMA((rows,)),
            pltpu.SemaphoreType.DMA((W_CHUNKS,)),
            pltpu.SemaphoreType.DMA((4,)),
        ],
        compiler_params=pltpu.CompilerParams(vmem_limit_bytes=63 * MIB),
        name="attend",
    )(place, length, query, fresh, routes, cache, weight)


def dispatch_kernel(
    base_ref,
    passed_ref,
    gain_ref,
    router_ref,
    hidden_ref,
    target_ref,
    gates_ref,
    slots_ref,
    row_buf,
    place_ref,
    place_sem,
    *,
    topk,
):
    batch, width = passed_ref.shape
    chunks = width // LANES
    target = jnp.concatenate(
        [base_ref[batch:, :LANES], base_ref[batch:, LANES : 2 * LANES]], axis=0
    ).astype(jnp.int32)
    target_ref[...] = target
    place_copy = pltpu.make_async_copy(target_ref, place_ref, place_sem)
    place_copy.start()
    hidden = base_ref[:batch, :] + passed_ref[...]
    hidden_ref[...] = hidden
    meansq = jnp.mean(hidden * hidden, axis=1, keepdims=True)
    normed = (hidden * lax.rsqrt(meansq + 1e-06) * gain_ref[...].astype(F32)).astype(BF16)
    for j in range(chunks):
        row_buf[pl.ds(j, batch, stride=chunks), :] = normed[
            :, j * LANES : (j + 1) * LANES
        ].astype(F32)

    raised = jnp.exp(dot(normed, router_ref[...]))
    routes = target // CAP
    lane = lax.broadcasted_iota(jnp.int32, (batch, LANES), 1)
    total = jnp.zeros((batch, 1), F32)
    gates = jnp.zeros((batch, LANES), F32)
    for k in range(topk):
        picked = jnp.sum(
            jnp.where(lane == routes[:, k : k + 1], raised, 0.0), axis=1, keepdims=True
        )
        total += picked
        gates = jnp.where(lane == k, picked, gates)
    gates_ref[...] = gates / total

    slots_ref[...] = jnp.zeros_like(slots_ref)
    place_copy.wait()
    for r in range(batch):
        row = row_buf[r * chunks : (r + 1) * chunks, :].astype(BF16)
        for k in range(topk):
            slots_ref[place_ref[r, k]] = row


def dispatch(base, passed, gain, router, topk):
    batch, width = passed.shape
    vmem = pl.BlockSpec(memory_space=pltpu.VMEM)
    return pl.pallas_call(
        functools.partial(dispatch_kernel, topk=topk),
        out_shape=(
            jax.ShapeDtypeStruct((batch, width), F32),
            jax.ShapeDtypeStruct((batch, LANES), jnp.int32),
            jax.ShapeDtypeStruct((batch, LANES), F32),
            jax.ShapeDtypeStruct((router.shape[1] * CAP, width // LANES, LANES), BF16),
        ),
        in_specs=[vmem] * 4,
        out_specs=(vmem, vmem, vmem, vmem),
        scratch_shapes=[
            pltpu.VMEM((batch * width // LANES, LANES), F32),
            pltpu.SMEM((batch, LANES), jnp.int32),
            pltpu.SemaphoreType.DMA,
        ],
        compiler_params=pltpu.CompilerParams(vmem_limit_bytes=SMALL_LIMIT),
        cost_estimate=pl.CostEstimate(
            flops=10_000_000_000, bytes_accessed=3_000_000, transcendentals=0
        ),
        name="dispatch",
    )(base, passed, gain, router)


def expert_kernel(x_ref, up_ref, down_ref, out_ref, served_buf, x_buf, act_buf):
    count, chunks, _ = x_ref.shape
    width = chunks * LANES
    step = STEP
    span = SPAN
    x_buf[...] = x_ref[...].reshape(count, width)
    for part in range(FF // step):
        gate = dot(x_buf[...], up_ref[:, part * step : (part + 1) * step])
        lift = dot(x_buf[...], up_ref[:, FF + part * step : FF + (part + 1) * step])
        act_buf[:, part * step : (part + 1) * step] = (
            gate * (1.0 / (1.0 + jnp.exp(-gate))) * lift
        ).astype(BF16)
    for part in range(width // span):
        served = dot(act_buf[...], down_ref[:, part * span : (part + 1) * span])
        served_buf[:, part * span : (part + 1) * span] = served.astype(BF16)
    out_ref[...] = served_buf[...].reshape(count, chunks, LANES)


def expert(x, up, down):
    count, chunks, _ = x.shape
    vmem = pl.BlockSpec(memory_space=pltpu.VMEM)
    return pl.pallas_call(
        expert_kernel,
        out_shape=jax.ShapeDtypeStruct(x.shape, BF16),
        in_specs=[vmem, vmem, vmem],
        out_specs=vmem,
        scratch_shapes=[
            pltpu.VMEM((count, chunks * LANES), BF16),
            pltpu.VMEM((count, chunks * LANES), BF16),
            pltpu.VMEM((count, FF), BF16),
        ],
        compiler_params=pltpu.CompilerParams(vmem_limit_bytes=EXPERT_LIMIT),
        name="expert",
    )(x, up, down)


def combine_kernel(target_ref, gates_ref, hidden_ref, table_ref, out_ref, row_buf, *, topk):
    batch, width = hidden_ref.shape
    chunks = width // LANES
    for r in range(batch):
        total = jnp.zeros((chunks, LANES), F32)
        for k in range(topk):
            total += gates_ref[r, k] * table_ref[target_ref[r, k]].astype(F32)
        row_buf[r * chunks : (r + 1) * chunks, :] = total
    for j in range(chunks):
        cols = slice(j * LANES, (j + 1) * LANES)
        out_ref[:, cols] = (
            hidden_ref[:, cols] + row_buf[pl.ds(j, batch, stride=chunks), :]
        ).astype(BF16)


def combine(target, gates, hidden, table, topk):
    batch, width = hidden.shape
    smem = pl.BlockSpec(memory_space=pltpu.SMEM)
    vmem = pl.BlockSpec(memory_space=pltpu.VMEM)
    return pl.pallas_call(
        functools.partial(combine_kernel, topk=topk),
        out_shape=jax.ShapeDtypeStruct((batch, width), BF16),
        in_specs=[smem, smem, vmem, vmem],
        out_specs=vmem,
        scratch_shapes=[pltpu.VMEM((batch * width // LANES, LANES), F32)],
        compiler_params=pltpu.CompilerParams(vmem_limit_bytes=SMALL_LIMIT),
        name="combine",
    )(target, gates, hidden, table)


def per_device(
    residual_in,
    queries,
    latest_key_value,
    key_value_cache,
    cache_len,
    out_weight,
    norm_gain,
    router_weight,
    routes,
    expert_gate_up,
    expert_down,
):
    rows = queries.shape[0] * queries.shape[1]
    experts = router_weight.shape[1]
    topk = routes.shape[1]
    place = lax.axis_index("grp").reshape(1)
    own, other = attend(
        place,
        cache_len,
        queries.reshape(rows, -1),
        latest_key_value.reshape((rows,) + latest_key_value.shape[2:]),
        routes.T,
        key_value_cache.reshape((rows,) + key_value_cache.shape[2:]),
        out_weight,
    )
    passed = lax.ppermute(other, "grp", [(0, 1), (1, 0)])
    below = own.shape[0] - residual_in.shape[0]
    base = jnp.pad(residual_in.astype(F32), ((0, below), (0, 0))) + own
    hidden, target, gates, slots = dispatch(
        base, passed, norm_gain.reshape(1, -1), router_weight, topk
    )
    block = (experts, CAP * slots.shape[1], LANES)
    received = lax.all_to_all(
        slots.reshape(block), ("grp", "dev"), split_axis=0, concat_axis=0, tiled=True
    )
    served = expert(received.reshape(slots.shape), expert_gate_up[0], expert_down[0])
    returned = lax.all_to_all(
        served.reshape(block), ("grp", "dev"), split_axis=0, concat_axis=0, tiled=True
    )
    return combine(target, gates, hidden, returned.reshape(slots.shape), topk)


def solution(mesh):
    placed = (
        P(("grp", "dev"), None),
        P(None, "dev", "grp"),
        P(None, "dev", "grp", None),
        P(None, "dev", "grp", None, None),
        P(None, "dev"),
        P("grp", None),
        P(),
        P(),
        P(("grp", "dev"), None),
        P(("grp", "dev"), None, None),
        P(("grp", "dev"), None, None),
    )
    return jax.shard_map(
        per_device, mesh=mesh, in_specs=placed, out_specs=P(("grp", "dev"), None), check_vma=False
    )
```

```python
import functools
import math

import jax
import jax.numpy as jnp
from jax import lax
from jax.experimental import pallas as pl
from jax.experimental.pallas import tpu as pltpu
from jax.sharding import PartitionSpec as P

HEAD_SIZE = 128
LANES = 128
FF = 768
CAP = 2
UNROLL = 8
WHOLE = 8
WSTEP = 0
TSTEP = 0
STEP = 256
SPAN = 512
W_CHUNKS = 4
NODMA=False
MIB = 1024 * 1024
SMALL_LIMIT = 12 * MIB
EXPERT_LIMIT = 24 * MIB

F32 = jnp.float32
BF16 = jnp.bfloat16


def dot(a, b, contract=((1,), (0,))):
    return lax.dot_general(a, b, (contract, ((), ())), preferred_element_type=F32)


def attend_kernel(
    place_ref,
    length_hbm,
    query_hbm,
    fresh_hbm,
    routes_hbm,
    cache_hbm,
    weight_hbm,
    own_ref,
    other_ref,
    cache_buf,
    weight_buf,
    query_ref,
    fresh_ref,
    routes_ref,
    length_ref,
    query_buf,
    fresh_buf,
    mixed_buf,
    cache_sem,
    weight_sem,
    small_sem,
):
    rows, kv_heads, positions, _ = cache_buf.shape
    q_heads = query_ref.shape[1] // HEAD_SIZE
    group = q_heads // kv_heads
    width = weight_buf.shape[1]
    span = width // W_CHUNKS
    half_rows = rows // 2
    scale = 1.0 / math.sqrt(HEAD_SIZE)

    def whole_copy(row):
        return pltpu.make_async_copy(cache_hbm.at[row], cache_buf.at[row], cache_sem.at[row])

    def part_copy(row):
        valid = length_ref[row // half_rows, row % half_rows]
        kept = pl.ds(0, pl.multiple_of((valid + 15) // 16 * 16, 16))
        return pltpu.make_async_copy(
            cache_hbm.at[row, :, kept], cache_buf.at[row, :, kept], cache_sem.at[row]
        )

    def weight_copy(part):
        cols = pl.ds(part * span, span)
        return pltpu.make_async_copy(
            weight_hbm.at[:, cols], weight_buf.at[:, cols], weight_sem.at[part]
        )

    length_copy = pltpu.make_async_copy(length_hbm, length_ref, small_sem.at[3])
    length_copy.start()
    small_copies = [
        pltpu.make_async_copy(source, kept, small_sem.at[i])
        for i, (source, kept) in enumerate(
            ((routes_hbm, routes_ref), (query_hbm, query_ref), (fresh_hbm, fresh_ref))
        )
    ]
    for copy in small_copies:
        copy.start()
    for row in range(WHOLE):
        whole_copy(row).start()
    for row in range(WHOLE, rows):
        cache_buf[row, :, :, HEAD_SIZE:] = jnp.zeros((kv_heads, positions, HEAD_SIZE), BF16)
    length_copy.wait()
    for row in range(WHOLE, rows):
        part_copy(row).start()

    for copy in small_copies:
        copy.wait()
    for j in range(q_heads):
        query_buf[pl.ds(j, rows, stride=q_heads), :] = query_ref[
            :, j * HEAD_SIZE : (j + 1) * HEAD_SIZE
        ].astype(F32)
    fresh_buf[...] = fresh_ref[...].astype(F32)

    def place_rows():
        topk, batch = routes_ref.shape
        unit = lax.broadcasted_iota(jnp.int32, (topk, topk), 0) == lax.broadcasted_iota(
            jnp.int32, (topk, topk), 1
        )
        routes = dot(
            routes_ref[...].astype(BF16), jnp.where(unit, 1.0, 0.0).astype(BF16), ((0,), (0,))
        ).astype(jnp.int32)
        lane = lax.broadcasted_iota(jnp.int32, (batch, LANES), 1)
        named = jnp.zeros((batch, LANES), F32)
        for k in range(topk):
            named += jnp.where(lane == routes[:, k : k + 1], 1.0, 0.0)
        below = lax.broadcasted_iota(jnp.int32, (batch, batch), 0) > lax.broadcasted_iota(
            jnp.int32, (batch, batch), 1
        )
        earlier = dot(jnp.where(below, 1.0, 0.0).astype(BF16), named.astype(BF16))
        slot = lane.astype(F32) * CAP + earlier
        target = jnp.zeros((batch, LANES), F32)
        for k in range(topk):
            found = jnp.sum(
                jnp.where(lane == routes[:, k : k + 1], slot, 0.0), axis=1, keepdims=True
            )
            target = jnp.where(lane == k, found, target)
        own_ref[batch:, :LANES] = target[: batch // 2]
        own_ref[batch:, LANES : 2 * LANES] = target[batch // 2 :]
        own_ref[batch:, 2 * LANES :] = jnp.zeros((batch // 2, width - 2 * LANES), F32)

    position = lax.broadcasted_iota(jnp.int32, (q_heads, positions), 1)

    def score(step):
        first = step * UNROLL
        query = query_buf[first * q_heads : (first + UNROLL) * q_heads, :]
        query16 = query.astype(BF16)
        scores, visible, new_key, new_value = [], [], [], []
        for u in range(UNROLL):
            fresh = fresh_buf[first + u]
            valid = length_ref[(first + u) // half_rows, (first + u) % half_rows]
            visible.append(position < valid)
            for head in range(kv_heads):
                begin = u * q_heads + head * group
                keys = cache_buf[first + u, head, :, :HEAD_SIZE]
                scores.append(dot(query16[begin : begin + group], keys, ((1,), (1,))))
                pair = jnp.broadcast_to(fresh[head : head + 1], (group, 2 * HEAD_SIZE))
                new_key.append(pair[:, :HEAD_SIZE])
                new_value.append(pair[:, HEAD_SIZE:])
        scores = jnp.concatenate(scores, axis=0) * scale
        new_key = jnp.concatenate(new_key, axis=0)
        own = jnp.exp(jnp.sum(query * new_key, axis=1, keepdims=True) * scale)
        raised = jnp.where(jnp.concatenate(visible, axis=0), jnp.exp(scores), 0.0)
        return raised, own, jnp.concatenate(new_value, axis=0)

    def mix(step, raised, own, new_value):
        first = step * UNROLL
        total = jnp.sum(raised, axis=1, keepdims=True) + own
        weights = (raised / total).astype(BF16)
        own_weight = (own / total).astype(BF16).astype(F32)
        mixed = []
        for u in range(UNROLL):
            for head in range(kv_heads):
                begin = u * q_heads + head * group
                values = cache_buf[first + u, head, :, HEAD_SIZE:]
                mixed.append(dot(weights[begin : begin + group], values))
        mixed = jnp.concatenate(mixed, axis=0) + own_weight * new_value
        mixed_buf[first * q_heads : (first + UNROLL) * q_heads, :] = mixed

    ready = None
    for step in range(rows // UNROLL):
        for u in range(UNROLL):
            row = step * UNROLL + u
            (whole_copy if row < WHOLE else part_copy)(row).wait()
        if step == WSTEP:
            for part in range(W_CHUNKS):
                weight_copy(part).start()
        if step == TSTEP:
            place_rows()
        scored = score(step)
        if step:
            mix(step - 1, *ready)
        ready = scored
    mix(step, *ready)

    attended = mixed_buf[...].astype(BF16).reshape(rows, q_heads * HEAD_SIZE)
    first_group = place_ref[0] == 0
    for part in range(W_CHUNKS):
        weight_copy(part).wait()
        cols = slice(part * span, (part + 1) * span)
        product = dot(attended, weight_buf[:, cols])
        top, bottom = product[: rows // 2], product[rows // 2 :]
        own_ref[:half_rows, cols] = jnp.where(first_group, top, bottom)
        other_ref[:, cols] = jnp.where(first_group, bottom, top)


def attend(place, length, query, fresh, routes, cache, weight):
    rows, kv_heads, positions, pair = cache.shape
    width = weight.shape[1]
    smem = pl.BlockSpec(memory_space=pltpu.SMEM)
    vmem = pl.BlockSpec(memory_space=pltpu.VMEM)
    hbm = pl.BlockSpec(memory_space=pltpu.HBM)
    half = rows // 2
    return pl.pallas_call(
        attend_kernel,
        out_shape=(
            jax.ShapeDtypeStruct((half + half // 2, width), F32),
            jax.ShapeDtypeStruct((half, width), F32),
        ),
        in_specs=[smem, hbm, hbm, hbm, hbm, hbm, hbm],
        out_specs=(vmem, vmem),
        scratch_shapes=[
            pltpu.VMEM(cache.shape, BF16),
            pltpu.VMEM(weight.shape, BF16),
            pltpu.VMEM(query.shape, BF16),
            pltpu.VMEM(fresh.shape, BF16),
            pltpu.VMEM(routes.shape, jnp.int32),
            pltpu.SMEM(length.shape, jnp.int32),
            pltpu.VMEM((rows * query.shape[1] // HEAD_SIZE, HEAD_SIZE), F32),
            pltpu.VMEM(fresh.shape, F32),
            pltpu.VMEM((rows * query.shape[1] // HEAD_SIZE, HEAD_SIZE), F32),
            pltpu.SemaphoreType.DMA((rows,)),
            pltpu.SemaphoreType.DMA((W_CHUNKS,)),
            pltpu.SemaphoreType.DMA((4,)),
        ],
        compiler_params=pltpu.CompilerParams(vmem_limit_bytes=63 * MIB),
        name="attend",
    )(place, length, query, fresh, routes, cache, weight)


def dispatch_kernel(
    base_ref,
    passed_ref,
    gain_ref,
    router_ref,
    hidden_ref,
    target_ref,
    gates_ref,
    slots_ref,
    row_buf,
    place_ref,
    place_sem,
    *,
    topk,
):
    batch, width = passed_ref.shape
    chunks = width // LANES
    target = jnp.concatenate(
        [base_ref[batch:, :LANES], base_ref[batch:, LANES : 2 * LANES]], axis=0
    ).astype(jnp.int32)
    target_ref[...] = target
    place_copy = pltpu.make_async_copy(target_ref, place_ref, place_sem)
    place_copy.start()
    hidden = base_ref[:batch, :] + passed_ref[...]
    hidden_ref[...] = hidden
    meansq = jnp.mean(hidden * hidden, axis=1, keepdims=True)
    normed = (hidden * lax.rsqrt(meansq + 1e-06) * gain_ref[...].astype(F32)).astype(BF16)
    row_buf[...] = normed.reshape(batch, chunks, LANES)

    raised = jnp.exp(dot(normed, router_ref[...]))
    routes = target // CAP
    lane = lax.broadcasted_iota(jnp.int32, (batch, LANES), 1)
    total = jnp.zeros((batch, 1), F32)
    gates = jnp.zeros((batch, LANES), F32)
    for k in range(topk):
        picked = jnp.sum(
            jnp.where(lane == routes[:, k : k + 1], raised, 0.0), axis=1, keepdims=True
        )
        total += picked
        gates = jnp.where(lane == k, picked, gates)
    gates_ref[...] = gates / total

    slots_ref[...] = jnp.zeros_like(slots_ref)
    place_copy.wait()
    for r in range(batch):
        row = row_buf[r]
        for k in range(topk):
            slots_ref[place_ref[r, k]] = row


def dispatch(base, passed, gain, router, topk):
    batch, width = passed.shape
    vmem = pl.BlockSpec(memory_space=pltpu.VMEM)
    return pl.pallas_call(
        functools.partial(dispatch_kernel, topk=topk),
        out_shape=(
            jax.ShapeDtypeStruct((batch, width), F32),
            jax.ShapeDtypeStruct((batch, LANES), jnp.int32),
            jax.ShapeDtypeStruct((batch, LANES), F32),
            jax.ShapeDtypeStruct((router.shape[1] * CAP, width // LANES, LANES), BF16),
        ),
        in_specs=[vmem] * 4,
        out_specs=(vmem, vmem, vmem, vmem),
        scratch_shapes=[
            pltpu.VMEM((batch, width // LANES, LANES), BF16),
            pltpu.SMEM((batch, LANES), jnp.int32),
            pltpu.SemaphoreType.DMA,
        ],
        compiler_params=pltpu.CompilerParams(vmem_limit_bytes=SMALL_LIMIT),
        cost_estimate=pl.CostEstimate(
            flops=10_000_000_000, bytes_accessed=3_000_000, transcendentals=0
        ),
        name="dispatch",
    )(base, passed, gain, router)


def expert_kernel(x_ref, up_ref, down_ref, out_ref, served_buf, x_buf, act_buf):
    count, chunks, _ = x_ref.shape
    width = chunks * LANES
    step = STEP
    span = SPAN
    x_buf[...] = x_ref[...].reshape(count, width)
    for part in range(FF // step):
        gate = dot(x_buf[...], up_ref[:, part * step : (part + 1) * step])
        lift = dot(x_buf[...], up_ref[:, FF + part * step : FF + (part + 1) * step])
        act_buf[:, part * step : (part + 1) * step] = (
            gate * (1.0 / (1.0 + jnp.exp(-gate))) * lift
        ).astype(BF16)
    for part in range(width // span):
        served = dot(act_buf[...], down_ref[:, part * span : (part + 1) * span])
        served_buf[:, part * span : (part + 1) * span] = served.astype(BF16)
    out_ref[...] = served_buf[...].reshape(count, chunks, LANES)


def expert(x, up, down):
    count, chunks, _ = x.shape
    vmem = pl.BlockSpec(memory_space=pltpu.VMEM)
    return pl.pallas_call(
        expert_kernel,
        out_shape=jax.ShapeDtypeStruct(x.shape, BF16),
        in_specs=[vmem, vmem, vmem],
        out_specs=vmem,
        scratch_shapes=[
            pltpu.VMEM((count, chunks * LANES), BF16),
            pltpu.VMEM((count, chunks * LANES), BF16),
            pltpu.VMEM((count, FF), BF16),
        ],
        compiler_params=pltpu.CompilerParams(vmem_limit_bytes=EXPERT_LIMIT),
        name="expert",
    )(x, up, down)


def combine_kernel(target_ref, gates_ref, hidden_ref, table_ref, out_ref, row_buf, *, topk):
    batch, width = hidden_ref.shape
    chunks = width // LANES
    for r in range(batch):
        total = jnp.zeros((chunks, LANES), F32)
        for k in range(topk):
            total += gates_ref[r, k] * table_ref[target_ref[r, k]].astype(F32)
        row_buf[r * chunks : (r + 1) * chunks, :] = total
    for j in range(chunks):
        cols = slice(j * LANES, (j + 1) * LANES)
        out_ref[:, cols] = (
            hidden_ref[:, cols] + row_buf[pl.ds(j, batch, stride=chunks), :]
        ).astype(BF16)


def combine(target, gates, hidden, table, topk):
    batch, width = hidden.shape
    smem = pl.BlockSpec(memory_space=pltpu.SMEM)
    vmem = pl.BlockSpec(memory_space=pltpu.VMEM)
    return pl.pallas_call(
        functools.partial(combine_kernel, topk=topk),
        out_shape=jax.ShapeDtypeStruct((batch, width), BF16),
        in_specs=[smem, smem, vmem, vmem],
        out_specs=vmem,
        scratch_shapes=[pltpu.VMEM((batch * width // LANES, LANES), F32)],
        compiler_params=pltpu.CompilerParams(vmem_limit_bytes=SMALL_LIMIT),
        name="combine",
    )(target, gates, hidden, table)


def per_device(
    residual_in,
    queries,
    latest_key_value,
    key_value_cache,
    cache_len,
    out_weight,
    norm_gain,
    router_weight,
    routes,
    expert_gate_up,
    expert_down,
):
    rows = queries.shape[0] * queries.shape[1]
    experts = router_weight.shape[1]
    topk = routes.shape[1]
    place = lax.axis_index("grp").reshape(1)
    own, other = attend(
        place,
        cache_len,
        queries.reshape(rows, -1),
        latest_key_value.reshape((rows,) + latest_key_value.shape[2:]),
        routes.T,
        key_value_cache.reshape((rows,) + key_value_cache.shape[2:]),
        out_weight,
    )
    passed = lax.ppermute(other, "grp", [(0, 1), (1, 0)])
    below = own.shape[0] - residual_in.shape[0]
    base = jnp.pad(residual_in.astype(F32), ((0, below), (0, 0))) + own
    hidden, target, gates, slots = dispatch(
        base, passed, norm_gain.reshape(1, -1), router_weight, topk
    )
    block = (experts, CAP * slots.shape[1], LANES)
    received = lax.all_to_all(
        slots.reshape(block), ("grp", "dev"), split_axis=0, concat_axis=0, tiled=True
    )
    served = expert(received.reshape(slots.shape), expert_gate_up[0], expert_down[0])
    returned = lax.all_to_all(
        served.reshape(block), ("grp", "dev"), split_axis=0, concat_axis=0, tiled=True
    )
    return combine(target, gates, hidden, returned.reshape(slots.shape), topk)


def solution(mesh):
    placed = (
        P(("grp", "dev"), None),
        P(None, "dev", "grp"),
        P(None, "dev", "grp", None),
        P(None, "dev", "grp", None, None),
        P(None, "dev"),
        P("grp", None),
        P(),
        P(),
        P(("grp", "dev"), None),
        P(("grp", "dev"), None, None),
        P(("grp", "dev"), None, None),
    )
    return jax.shard_map(
        per_device, mesh=mesh, in_specs=placed, out_specs=P(("grp", "dev"), None), check_vma=False
    )
```
